128 devices in a mesh: row: 32 (over x, y, core), col: 4 (over z).
Axes of the slice: x: 4, y: 4, z: 4, core: 2. Of those that a mesh axis runs over, the one named last changes fastest.
Arguments:
- front_matrix: float32 [12288, 16384], P('row', 'col'), may hold values from -6 to 6
- child_rows: float32 [2048, 16384], P('row', 'col'), may hold values from -6 to 6
- child_owner: int32 [2048, 1], P('row'), may hold values from 0 to 31; in each aligned block of 64 rows (0 to 63, 64 to 127, ...) at most 4 rows name the same one
- child_offset: int32 [2048, 1], P('row'), may hold values from 0 to 383
Outputs:
- upper_rows: float32 [512, 16384], P(None, 'col')
- reduced_front: float32 [12288, 16384], P('row', 'col')
- basis_scaled: float32 [12288, 512], P('row')
The draws below stay inside these ranges and needn't reach their ends.
Inputs may be any that keep to these rules, and one draw needn't show every extreme that they name: `child_owner`: within the rows of one device (aligned blocks of 64 rows) no value occurs more than 4 times, and some value occurs exactly 4 times.
All inputs are finite; a program needn't handle non-finite values.
Results may differ from the reference program's by a relative error of at most 0.0001.
Values sent between devices are 32-bit elements; how exact they have to be, the bound alone decides.
A program may use at most 128 MiB of HBM per device.

```python
import math
import jax
import jax.numpy as jnp
import numpy as np
from jax import lax

NC = 16384
PB = 128
PANELS = 4
ROWS_DEV = 384
CHILD_DEV = 64
M = 12288
CHILDREN = 2048
MOST = 4
N_ROW = 32


def touch_ends(drawn, key, smallest, largest):
    index_at = [jax.random.randint(jax.random.fold_in(key, axis), (), 0, length) for axis, length in enumerate(drawn.shape)]
    main_axis = drawn.shape.index(max(drawn.shape))
    beside = index_at[:main_axis] + [(index_at[main_axis] + 1) % drawn.shape[main_axis]] + index_at[main_axis + 1:]
    return drawn.at[tuple(index_at)].set(smallest).at[tuple(beside)].set(largest)


def steps_of(own_key, extent, cuts, smallest, largest):
    def one(dim, parts):
        draws = jax.random.uniform(jax.random.fold_in(jax.random.fold_in(own_key, 6), dim), (parts,), jnp.float32, smallest / len(cuts), largest / len(cuts))
        return jnp.repeat(jnp.exp(draws), extent[dim] // parts).reshape((-1,) + (1,) * (len(extent) - dim - 1))

    factor_of = one(*cuts[0])
    for cut in cuts[1:]:
        factor_of = factor_of * one(*cut)
    return factor_of


def assign_block(rng, own, number, rows, count, top, limit, skew):
    order = jax.random.permutation(rng, count)
    packed, common = portions_of(count, rows * top, limit, skew, True), portions_of(count, rows * top, limit, skew, False)
    places = jnp.arange(count)

    def named(tallies, offset_by):
        used = int((tallies > 0).sum())
        fixed = max(1, used // 4)
        passed = fixed + (places - fixed + offset_by * (used - fixed)) % max(1, count - fixed)
        return jnp.zeros((count,), jnp.int32).at[order[jnp.where(places < fixed, places, passed)]].set(jnp.asarray(tallies, jnp.int32))

    tallies = jnp.where(number % 4 == 0, named(packed, number // 4), named(common, number - number // 4 - 1))
    mixed = jax.random.permutation(jax.random.fold_in(own, 3), count)
    donor, sink = mixed[0:count // 2 * 2:2], mixed[1:count // 2 * 2:2]
    room = jnp.minimum(tallies[donor] - 1, limit - tallies[sink]) // 2
    room = jnp.where((donor == order[0]) | (sink == order[0]) | (tallies[sink] == 0), 0, jnp.maximum(room, 0))
    passed = jax.random.randint(jax.random.fold_in(own, 4), (count // 2,), 0, 1 << 20) % (room + 1)
    tallies = tallies.at[donor].add(-passed).at[sink].add(passed)
    members = jnp.searchsorted(jnp.cumsum(tallies), jnp.arange(rows * top), side="right").astype(jnp.int32)
    grid = members.reshape(top, rows).T
    grid = grid[jax.random.permutation(jax.random.fold_in(own, 1), rows)]
    offset_by = jax.random.randint(jax.random.fold_in(own, 2), (rows, 1), 0, top)
    return jnp.take_along_axis(grid, (jnp.arange(top)[None, :] + offset_by) % top, axis=1)


def portions_of(number_of, total, most, skew, full):
    weights = [(1 << 20) // math.isqrt(rank ** skew) + 1 for rank in range(1, number_of + 1)]
    largest = most if full else min(most, max(-(-total // number_of), total * weights[0] // sum(weights)))
    least = 1 if total - largest >= number_of - 1 else 0
    given, surplus = [largest] + [least] * (number_of - 1), total - largest - least * (number_of - 1)
    while surplus > 0:
        movable = [i for i in range(1, number_of) if given[i] < largest] or [i for i in range(1, number_of) if given[i] < most]
        whole, left = sum([weights[i] for i in movable]), surplus
        for i in movable:
            addition = min(most - given[i], max(1, left * weights[i] // whole), surplus)
            given[i] = given[i] + addition
            surplus = surplus - addition
    return np.array(given)


def noise(key, shape, scale, reach, shards=(), kind=jnp.bfloat16):
    loudness = steps_of(key, shape, shards, -0.22, 0.18) if shards else 1.0
    result = jax.random.normal(key, shape, jnp.float32) * scale * loudness
    return jnp.minimum(jnp.maximum(result, -reach), reach).astype(kind)


def setup_inputs(seed: int = 0) -> dict:
    streams_of = jax.random.split(jax.random.key(seed), 5)
    front_matrix = noise(streams_of[0], (M, NC), 1.0, 6.0, ((0, 32), (1, 4)), jnp.float32)
    child_rows = noise(streams_of[1], (CHILDREN, NC), 1.0, 6.0, ((0, 32), (1, 4)), jnp.float32)
    child_owner_keys = jax.random.split(jax.random.fold_in(streams_of[2], 1), CHILDREN // CHILD_DEV)
    child_owner_turns = jax.random.permutation(jax.random.fold_in(streams_of[2], 3), CHILDREN // CHILD_DEV)
    child_owner = jax.vmap(lambda own, number: assign_block(jax.random.fold_in(streams_of[2], 2), own, number, CHILD_DEV, N_ROW, 1, MOST, 1))(child_owner_keys, child_owner_turns).reshape((CHILDREN, 1))
    child_offset = touch_ends(jax.random.randint(streams_of[3], (CHILDREN, 1), 0, ROWS_DEV), jax.random.fold_in(streams_of[3], 1), 0, ROWS_DEV - 1).astype(jnp.int32)
    return {"front_matrix": front_matrix, "child_rows": child_rows, "child_owner": child_owner, "child_offset": child_offset}


def product(left_op, right_op):
    return jnp.dot(left_op.astype(jnp.float32), right_op.astype(jnp.float32), precision=lax.Precision.HIGHEST, preferred_element_type=jnp.float32)

def factor_panel(panel_cols):
    gram_total = product(panel_cols.T, panel_cols)
    lower_factor = jnp.linalg.cholesky(gram_total)
    return lax.linalg.triangular_solve(lower_factor, panel_cols, left_side=False, lower=True, transpose_a=True)

def reference(front_matrix, child_rows, child_owner, child_offset):
    target = (child_owner[:, 0] * ROWS_DEV + child_offset[:, 0]).astype(jnp.int32)
    current = front_matrix.at[target].add(child_rows)
    top_list = []
    basis_list = []
    for panel_index in range(PANELS):
        basis = factor_panel(current[:, panel_index * PB:(panel_index + 1) * PB])
        top_rows = product(basis.T, current)
        current = current - product(basis, top_rows)
        top_list.append(top_rows)
        basis_list.append(basis)
    scaled = jnp.concatenate(basis_list, axis=1) * math.sqrt(M)
    return (jnp.concatenate(top_list, axis=0), current, scaled)
```

```python
import math

import jax
import jax.numpy as jnp
from jax import lax
from jax.sharding import PartitionSpec as P

PB = 128
PANELS = 4
WIDE = PB * PANELS


def product(left_op, right_op):
    return jnp.dot(
        left_op, right_op, precision=lax.Precision.HIGHEST, preferred_element_type=jnp.float32
    )


def from_first(block, axis):
    count = lax.axis_size(axis)
    me = lax.axis_index(axis)
    out = block
    for peer in range(1, count):
        got = lax.ppermute(block, axis, [(0, peer)])
        out = jnp.where(me == peer, got, out)
    return out


def on_device(front_matrix, child_rows, child_owner, child_offset):
    row_count = lax.axis_size("row")
    local_rows = front_matrix.shape[0]
    local_cols = front_matrix.shape[1]
    child_count = child_rows.shape[0]
    capacity = 2 * child_count // row_count
    slot_total = row_count * capacity
    owner_rows = child_owner[:, 0]
    onehot = (owner_rows[:, None] == jnp.arange(row_count, dtype=jnp.int32)[None, :]).astype(
        jnp.int32
    )
    rank_in = jnp.sum(onehot * (jnp.cumsum(onehot, axis=0) - 1), axis=1)
    position = owner_rows * capacity + rank_in
    sender = jnp.zeros((slot_total, local_cols), jnp.float32).at[position].set(child_rows)
    offsets = jnp.full((slot_total,), local_rows, jnp.int32).at[position].set(child_offset[:, 0])
    received, placed = (
        lax.all_to_all(
            sender.reshape(row_count, capacity, local_cols),
            "row",
            split_axis=0,
            concat_axis=0,
            tiled=True,
        ),
        lax.all_to_all(
            offsets.reshape(row_count, capacity), "row", split_axis=0, concat_axis=0, tiled=True
        ),
    )
    current = front_matrix.at[placed.reshape(slot_total)].add(
        received.reshape(slot_total, local_cols), mode="drop"
    )
    panel = from_first(current[:, :WIDE], "col")
    inner = lax.psum(product(panel.T, current), "row")
    gram = from_first(inner[:, :WIDE], "col")
    lower_factor = jnp.linalg.cholesky(gram)
    inverse = lax.linalg.triangular_solve(
        lower_factor, jnp.eye(WIDE, dtype=jnp.float32), left_side=True, lower=True
    )
    upper = product(inverse, inner)
    basis = product(panel, inverse.T)
    reduced = current - product(basis, upper)
    total_rows = local_rows * row_count
    return (upper, reduced, basis * math.sqrt(total_rows))


def solution(mesh):
    placed = (P("row", "col"), P("row", "col"), P("row", None), P("row", None))
    return jax.shard_map(
        on_device,
        mesh=mesh,
        in_specs=placed,
        out_specs=(P(None, "col"), P("row", "col"), P("row", None)),
        check_vma=False,
    )
```

```python
import functools
import math

import jax
import jax.numpy as jnp
from jax import lax
from jax.experimental import pallas as pl
from jax.experimental.pallas import tpu as pltpu
from jax.sharding import PartitionSpec as P

PB = 128
PANELS = 4
WIDE = PB * PANELS
MESH = pl.DeviceIdType.MESH
F32 = jnp.float32
BF16 = jnp.bfloat16
SIDE = 4
HALF = WIDE // 2
SHARD = HALF // SIDE
SUB = SHARD // SIDE
CW = 1024
COPIES = 22


def product(left_op, right_op):
    return jnp.dot(
        left_op, right_op, precision=lax.Precision.HIGHEST, preferred_element_type=F32
    )


def split(value):
    high = value.astype(BF16)
    return high, (value - high.astype(F32)).astype(BF16)


def dot3(lh, ll, rh, rl):
    def one(a, b):
        return jnp.dot(a, b, preferred_element_type=F32)

    return one(lh, rh) + (one(lh, rl) + one(ll, rh))


def chol_steps(dblk, xblk, start, stop):
    lane = lax.broadcasted_iota(jnp.int32, (PB, PB), 1)
    sub = lax.broadcasted_iota(jnp.int32, (PB, PB), 0)

    def step(j, carry):
        a = dblk[...]
        x = xblk[...]
        row = dblk[pl.ds(j, 1), :]
        xrow = xblk[pl.ds(j, 1), :]
        col = jnp.sum(jnp.where(lane == j, a, 0.0), axis=1, keepdims=True)
        piv = jnp.sum(
            jnp.where(lax.broadcasted_iota(jnp.int32, (1, PB), 1) == j, row, 0.0),
            axis=1,
            keepdims=True,
        )
        inv = 1.0 / jnp.sqrt(piv)
        below = sub > j
        here = sub == j
        mult = col * (inv * inv)
        dblk[...] = jnp.where(below, a - mult * row, a)
        xblk[...] = jnp.where(below, x - mult * xrow, jnp.where(here, x * inv, x))
        return carry

    lax.fori_loop(start, stop, step, 0)


def tdot(a, b):
    return lax.dot_general(
        a, b, (((1,), (1,)), ((), ())), precision=lax.Precision.HIGHEST, preferred_element_type=F32
    )


def main_kernel(
    a1_ref, a1t_ref, w_ref, f_ref, linv_ref,
    p_ref, ah, al, r0, r1, r2, g_ref, dblk, xblk, lcol,
    send_sem, recv_sem,
):
    r = lax.axis_index("row")
    core = lax.rem(r, 2)
    yy = lax.rem(r // 2, SIDE)
    xx = r // (2 * SIDE)
    other = 1 - core
    a = other * xx + core * yy
    b = core * xx + other * yy

    def at(first, second):
        px = other * first + core * second
        py = core * first + other * second
        return (px * SIDE + py) * 2 + core

    a_up, a_dn, a_op = lax.rem(a + 1, SIDE), lax.rem(a + 3, SIDE), lax.rem(a + 2, SIDE)
    b_up, b_dn, b_op = lax.rem(b + 1, SIDE), lax.rem(b + 3, SIDE), lax.rem(b + 2, SIDE)
    partner = r + 1 - 2 * core
    dev = {
        "p": partner,
        "a+": at(a_up, b),
        "a-": at(a_dn, b),
        "b+": at(a, b_up),
        "b-": at(a, b_dn),
    }
    barrier = pltpu.get_barrier_semaphore()
    for peer in dev.values():
        pl.semaphore_signal(barrier, inc=1, device_id={"row": peer}, device_id_type=MESH)
    pl.semaphore_wait(barrier, len(dev))

    total_cols = w_ref.shape[1]
    chunks = [(0, WIDE)] + [(WIDE + i * CW, CW) for i in range(total_cols // CW)]
    n = len(chunks)
    started = {}

    def send(c, slot, src, dst, where):
        copy = pltpu.make_async_remote_copy(
            src_ref=src,
            dst_ref=dst,
            send_sem=send_sem.at[c, slot],
            recv_sem=recv_sem.at[c, slot],
            device_id={"row": dev[where]},
            device_id_type=MESH,
        )
        copy.start()
        started[(c, slot)] = copy

    def got(c, slot):
        started[(c, slot)].wait_recv()

    own = HALF * core

    def mult8(v, m=8):
        return pl.multiple_of(v, m)

    def shard(i, half=0):
        return mult8(own + SHARD * i + half * (SHARD // 2))

    def sub(i, half=0):
        return mult8(own + SHARD * a + SUB * i + half * (SUB // 2))

    def fill(c):
        c0, cw = chunks[c]
        if c == 0:
            p_ref[:, pl.ds(0, WIDE)] = product(a1t_ref[...], a1_ref[...])
            hi, lo = split(a1t_ref[...])
            ah[...] = hi
            al[...] = lo
            return

        def tile(i, carry):
            off = pl.multiple_of(c0 - WIDE + i * 256, 256)
            wh, wl = split(w_ref[:, pl.ds(off, 256)])
            p_ref[:, pl.ds(pl.multiple_of(off + WIDE, 256), 256)] = dot3(ah[...], al[...], wh, wl)
            return carry

        lax.fori_loop(0, cw // 256, tile, 0)

    def phase(c, p):
        c0, cw = chunks[c]
        cols = pl.ds(c0, cw)

        def part(row, count):
            return p_ref.at[pl.ds(row, count), cols]

        def full(row, count):
            return f_ref.at[pl.ds(row, count), cols]

        def add(row, count, *sources):
            rows = pl.ds(row, count)
            value = p_ref[rows, cols]
            for source in sources:
                value = value + source[...]
            p_ref[rows, cols] = value

        s32, s8 = SHARD // 2, SUB // 2
        one = lambda i: r1.at[pl.ds(i * s32, s32), cols]
        two = lambda i: r2.at[pl.ds(i * s8, s8), cols]
        if p == 0:
            fill(c)
            there = mult8(HALF * other)
            send(c, 0, part(there, HALF), r0.at[:, cols], "p")
        elif p == 1:
            got(c, 0)
            add(mult8(own), HALF, r0.at[:, cols])
            send(c, 1, part(shard(a_op, 0), s32), one(0), "a+")
            send(c, 2, part(shard(a_op, 1), s32), one(1), "a-")
            send(c, 3, part(shard(a_up, 1), s32), one(2), "a+")
            send(c, 4, part(shard(a_dn, 0), s32), one(3), "a-")
        elif p == 2:
            got(c, 1)
            add(shard(a_up, 0), s32, one(0))
            send(c, 5, part(shard(a_up, 0), s32), one(4), "a+")
            got(c, 2)
            add(shard(a_dn, 1), s32, one(1))
            send(c, 6, part(shard(a_dn, 1), s32), one(5), "a-")
        elif p == 3:
            for slot in (3, 4, 5, 6):
                got(c, slot)
            add(shard(a, 0), s32, one(3), one(4))
            add(shard(a, 1), s32, one(2), one(5))
            send(c, 7, part(sub(b_op, 0), s8), two(0), "b+")
            send(c, 8, part(sub(b_op, 1), s8), two(1), "b-")
            send(c, 9, part(sub(b_up, 1), s8), two(2), "b+")
            send(c, 10, part(sub(b_dn, 0), s8), two(3), "b-")
        elif p == 4:
            got(c, 7)
            add(sub(b_up, 0), s8, two(0))
            send(c, 11, part(sub(b_up, 0), s8), two(4), "b+")
            got(c, 8)
            add(sub(b_dn, 1), s8, two(1))
            send(c, 12, part(sub(b_dn, 1), s8), two(5), "b-")
        elif p == 5:
            for slot in (9, 10, 11, 12):
                got(c, slot)
            f_ref[pl.ds(sub(b, 0), s8), cols] = (
                p_ref[pl.ds(sub(b, 0), s8), cols] + two(3)[...] + two(4)[...]
            )
            f_ref[pl.ds(sub(b, 1), s8), cols] = (
                p_ref[pl.ds(sub(b, 1), s8), cols] + two(2)[...] + two(5)[...]
            )
            send(c, 13, full(sub(b), SUB), full(sub(b), SUB), "b+")
            send(c, 14, full(sub(b), SUB), full(sub(b), SUB), "b-")
        elif p == 6:
            got(c, 13)
            send(c, 15, full(sub(b_dn, 0), s8), full(sub(b_dn, 0), s8), "b+")
            got(c, 14)
            send(c, 16, full(sub(b_up, 1), s8), full(sub(b_up, 1), s8), "b-")
        elif p == 7:
            got(c, 15)
            got(c, 16)
            send(c, 17, full(shard(a), SHARD), full(shard(a), SHARD), "a+")
            send(c, 18, full(shard(a), SHARD), full(shard(a), SHARD), "a-")
        elif p == 8:
            got(c, 17)
            send(c, 19, full(shard(a_dn, 0), s32), full(shard(a_dn, 0), s32), "a+")
            got(c, 18)
            send(c, 20, full(shard(a_up, 1), s32), full(shard(a_up, 1), s32), "a-")
        elif p == 9:
            got(c, 19)
            got(c, 20)
            send(c, 21, full(mult8(own), HALF), full(mult8(own), HALF), "p")
        elif p == 10:
            got(c, 21)

    def chol_begin(k):
        if k == 0:
            g_ref[...] = f_ref[:, pl.ds(0, WIDE)]
            linv_ref[...] = jnp.zeros_like(linv_ref)
        d = pl.ds(k * PB, PB)
        dblk[...] = g_ref[d, d]
        xblk[...] = jnp.where(
            lax.broadcasted_iota(jnp.int32, (PB, PB), 0)
            == lax.broadcasted_iota(jnp.int32, (PB, PB), 1),
            1.0,
            0.0,
        ).astype(F32)

    def chol_end(k):
        d = pl.ds(k * PB, PB)
        x = xblk[...]
        if k:
            left = pl.ds(0, k * PB)
            linv_ref[d, left] = -product(x, product(g_ref[d, left], linv_ref[left, left]))
        linv_ref[d, d] = x
        if k < PANELS - 1:
            rest = pl.ds((k + 1) * PB, (PANELS - 1 - k) * PB)
            below = tdot(g_ref[rest, d], x)
            g_ref[rest, d] = below
            g_ref[rest, rest] = g_ref[rest, rest] - tdot(below, below)

    pieces = []
    for k in range(PANELS):
        for q in range(2):
            pieces.append((k, q))

    def piece(k, q):
        if q == 0:
            chol_begin(k)
        chol_steps(dblk, xblk, q * (PB // 2), (q + 1) * (PB // 2))
        if q == 1:
            chol_end(k)

    last = 2 * (n - 1) + 10
    nxt = 0
    for t in range(last + 1):
        for c in range(n):
            p = t - 2 * c
            if 0 <= p <= 10:
                phase(c, p)
        if t >= 10 and nxt < len(pieces):
            piece(*pieces[nxt])
            nxt += 1
    while nxt < len(pieces):
        piece(*pieces[nxt])
        nxt += 1
    for copy in started.values():
        copy.wait_send()


def all_reduced(a1, a1t, w):
    rows, cols = w.shape
    wide = cols + WIDE
    n = 1 + cols // CW
    vm = pl.BlockSpec(memory_space=pltpu.VMEM)
    return pl.pallas_call(
        main_kernel,
        out_shape=(
            jax.ShapeDtypeStruct((WIDE, wide), F32),
            jax.ShapeDtypeStruct((WIDE, WIDE), F32),
        ),
        in_specs=[vm] * 3,
        out_specs=(vm, vm),
        scratch_shapes=[
            pltpu.VMEM((WIDE, wide), F32),
            pltpu.VMEM((WIDE, rows), BF16),
            pltpu.VMEM((WIDE, rows), BF16),
            pltpu.VMEM((HALF, wide), F32),
            pltpu.VMEM((6 * SHARD // 2, wide), F32),
            pltpu.VMEM((6 * SUB // 2, wide), F32),
            pltpu.VMEM((WIDE, WIDE), F32),
            pltpu.VMEM((PB, PB), F32),
            pltpu.VMEM((PB, PB), F32),
            pltpu.VMEM((PB, PB), F32),
            pltpu.SemaphoreType.DMA((n, COPIES)),
            pltpu.SemaphoreType.DMA((n, COPIES)),
        ],
        compiler_params=pltpu.CompilerParams(
            collective_id=0, has_side_effects=True, vmem_limit_bytes=60 * 1024 * 1024
        ),
        name="all_reduce_gram",
    )(a1, a1t, w)


def tail_kernel(scale, a1_ref, linv_ref, s_ref, w_ref, u_ref, o_ref, q_ref, lh, ll, qh, ql):
    @pl.when(pl.program_id(0) == 0)
    def _():
        linv = linv_ref[...]
        hi, lo = split(linv)
        lh[...] = hi
        ll[...] = lo
        basis = tdot(a1_ref[...], linv)
        q_ref[...] = basis * scale
        hi, lo = split(basis)
        qh[...] = hi
        ql[...] = lo

    sh, sl = split(s_ref[...])
    u = dot3(lh[...], ll[...], sh, sl)
    u_ref[...] = u
    uh, ul = split(u)
    o_ref[...] = w_ref[...] - dot3(qh[...], ql[...], uh, ul)


def tail(a1, linv, sums, w, scale):
    rows, cols = w.shape
    tc = 512
    off = WIDE // tc
    whole = lambda shape: pl.BlockSpec(shape, lambda i: (0, 0))
    return pl.pallas_call(
        functools.partial(tail_kernel, scale),
        grid=(cols // tc,),
        out_shape=(
            jax.ShapeDtypeStruct((WIDE, cols), F32),
            jax.ShapeDtypeStruct((rows, cols), F32),
            jax.ShapeDtypeStruct((rows, WIDE), F32),
        ),
        in_specs=[
            whole((rows, WIDE)),
            whole((WIDE, WIDE)),
            pl.BlockSpec((WIDE, tc), lambda i: (0, i + off)),
            pl.BlockSpec((rows, tc), lambda i: (0, i)),
        ],
        out_specs=(
            pl.BlockSpec((WIDE, tc), lambda i: (0, i)),
            pl.BlockSpec((rows, tc), lambda i: (0, i)),
            whole((rows, WIDE)),
        ),
        scratch_shapes=[
            pltpu.VMEM((WIDE, WIDE), BF16),
            pltpu.VMEM((WIDE, WIDE), BF16),
            pltpu.VMEM((rows, WIDE), BF16),
            pltpu.VMEM((rows, WIDE), BF16),
        ],
        compiler_params=pltpu.CompilerParams(vmem_limit_bytes=40 * 1024 * 1024),
        name="project_out",
    )(a1, linv, sums, w)


def from_first(block, axis):
    count = lax.axis_size(axis)
    me = lax.axis_index(axis)
    out = block
    for peer in range(1, count):
        got = lax.ppermute(block, axis, [(0, peer)])
        out = jnp.where(me == peer, got, out)
    return out


def on_device(front_matrix, child_rows, child_owner, child_offset):
    row_count = lax.axis_size("row")
    local_rows = front_matrix.shape[0]
    local_cols = front_matrix.shape[1]
    child_count = child_rows.shape[0]
    capacity = 2 * child_count // row_count
    slot_total = row_count * capacity
    owner_rows = child_owner[:, 0]
    onehot = (owner_rows[:, None] == jnp.arange(row_count, dtype=jnp.int32)[None, :]).astype(
        jnp.int32
    )
    rank_in = jnp.sum(onehot * (jnp.cumsum(onehot, axis=0) - 1), axis=1)
    position = owner_rows * capacity + rank_in
    sender = jnp.zeros((slot_total, local_cols), jnp.float32).at[position].set(child_rows)
    offsets = jnp.full((slot_total,), local_rows, jnp.int32).at[position].set(child_offset[:, 0])
    received, placed = (
        lax.all_to_all(
            sender.reshape(row_count, capacity, local_cols),
            "row",
            split_axis=0,
            concat_axis=0,
            tiled=True,
        ),
        lax.all_to_all(
            offsets.reshape(row_count, capacity), "row", split_axis=0, concat_axis=0, tiled=True
        ),
    )
    current = front_matrix.at[placed.reshape(slot_total)].add(
        received.reshape(slot_total, local_cols), mode="drop"
    )
    panel = from_first(current[:, :WIDE], "col")
    sums, linv = all_reduced(panel, panel.T, current)
    return tail(panel, linv, sums, current, math.sqrt(local_rows * row_count))


def solution(mesh):
    placed = (P("row", "col"), P("row", "col"), P("row", None), P("row", None))
    return jax.shard_map(
        on_device,
        mesh=mesh,
        in_specs=placed,
        out_specs=(P(None, "col"), P("row", "col"), P("row", None)),
        check_vma=False,
    )
```

```python
import functools
import math

import jax
import jax.numpy as jnp
from jax import lax
from jax.experimental import pallas as pl
from jax.experimental.pallas import tpu as pltpu
from jax.sharding import PartitionSpec as P

PB = 128
PANELS = 4
WIDE = PB * PANELS
MESH = pl.DeviceIdType.MESH
F32 = jnp.float32
BF16 = jnp.bfloat16
SIDE = 4
HALF = WIDE // 2
SHARD = HALF // SIDE
SUB = SHARD // SIDE
CW = 512
HC = 256
TAG = 128
GROUP = 4
GRAM_TAU = (-2, -1, 2, 3, 4, 5, 6)
PIECES = 4
COPIES = 22
ZROWS = 32


def product(left_op, right_op):
    return jnp.dot(
        left_op, right_op, precision=lax.Precision.HIGHEST, preferred_element_type=F32
    )


def split(value):
    high = value.astype(BF16)
    return high, (value - high.astype(F32)).astype(BF16)


def split3(value):
    high = value.astype(BF16)
    rest = value - high.astype(F32)
    mid = rest.astype(BF16)
    return high, mid, (rest - mid.astype(F32)).astype(BF16)


def place(onehot, value):
    high, mid, low = split3(value)

    def one(part):
        return jnp.dot(onehot, part, preferred_element_type=F32)

    return one(high) + (one(mid) + one(low))


def dot3(lh, ll, rh, rl):
    def one(a, b):
        return jnp.dot(a, b, preferred_element_type=F32)

    return one(lh, rh) + (one(lh, rl) + one(ll, rh))


def chol_steps(dblk, xblk, start, stop):
    lane = lax.broadcasted_iota(jnp.int32, (PB, PB), 1)
    lane1 = lax.broadcasted_iota(jnp.int32, (1, PB), 1)
    sub = lax.broadcasted_iota(jnp.int32, (PB, PB), 0)

    def step(i, carry):
        j = i * GROUP
        a, x = dblk[...], xblk[...]
        span = range(GROUP)
        rows = [dblk[pl.ds(j + q, 1), :] for q in span]
        xrows = [xblk[pl.ds(j + q, 1), :] for q in span]
        cols = [
            jnp.sum(jnp.where(lane == j + q, a, 0.0), axis=1, keepdims=True) for q in span
        ]
        m = {
            (p, q): jnp.sum(jnp.where(lane1 == j + q, rows[p], 0.0), axis=1, keepdims=True)
            for p in span
            for q in range(p, GROUP)
        }
        invs = []
        for p in span:
            inv = lax.rsqrt(m[p, p])
            inv2 = inv * inv
            invs.append(inv)
            for q in range(p + 1, GROUP):
                f = m[p, q] * inv2
                rows[q] = rows[q] - f * rows[p]
                xrows[q] = xrows[q] - f * xrows[p]
                cols[q] = cols[q] - f * cols[p]
                for r in range(q, GROUP):
                    m[q, r] = m[q, r] - f * m[p, r]
            cols[p] = cols[p] * inv2
        below = sub > j + GROUP - 1
        na, nx = a, x
        for p in span:
            na = na - cols[p] * rows[p]
            nx = nx - cols[p] * xrows[p]
        nx = jnp.where(below, nx, x)
        for p in span:
            nx = jnp.where(sub == j + p, xrows[p] * invs[p], nx)
        dblk[...] = jnp.where(below, na, a)
        xblk[...] = nx
        return carry

    lax.fori_loop(start // GROUP, stop // GROUP, step, 0)


def tdot(a, b):
    return lax.dot_general(
        a, b, (((1,), (1,)), ((), ())), precision=lax.Precision.HIGHEST, preferred_element_type=F32
    )


def main_kernel(
    child_ref, ocol_ref, orow_ref, off_ref, front_ref,
    w_out, f_out, a1_out, linv_ref,
    w_ref, f_ref, p_ref, a1_ref, ah, al, r0, r1, r2, g_ref, dblk, xblk,
    outbox, inbox, onehot,
    send_sem, recv_sem, box_send, box_recv, z_send, z_recv, local_sem,
):
    count = lax.axis_size("row")
    deep = lax.axis_size("col")
    r = lax.axis_index("row")
    z = lax.axis_index("col")
    core = lax.rem(r, 2)
    yy = lax.rem(r // 2, SIDE)
    xx = r // (2 * SIDE)
    other = 1 - core
    a = other * xx + core * yy
    b = core * xx + other * yy
    rows, total_cols = w_ref.shape
    kids = child_ref.shape[0]

    def mult8(v, m=8):
        return pl.multiple_of(v, m)

    def at(first, second):
        px = other * first + core * second
        py = core * first + other * second
        return (px * SIDE + py) * 2 + core

    load = pltpu.make_async_copy(front_ref, w_ref, local_sem.at[0])
    load.start()

    barrier = pltpu.get_barrier_semaphore()

    def greet(d, carry):
        pl.semaphore_signal(
            barrier, inc=1, device_id={"row": lax.rem(r + d, count)}, device_id_type=MESH
        )
        return carry

    lax.fori_loop(1, count, greet, 0)
    z_up, z_dn = lax.rem(z + 1, deep), lax.rem(z + deep - 1, deep)
    for peer in (z_up, z_dn):
        pl.semaphore_signal(barrier, inc=1, device_id={"col": peer}, device_id_type=MESH)

    orow = orow_ref[...]
    earlier = lax.broadcasted_iota(jnp.int32, (kids, kids), 0) < lax.broadcasted_iota(
        jnp.int32, (kids, kids), 1
    )
    same = jnp.logical_and(ocol_ref[...] == orow, earlier)
    rank = jnp.sum(jnp.where(same, 1.0, 0.0), axis=0, keepdims=True).astype(jnp.int32)
    slot = orow * 8 + rank * 2
    boxes = 8 * count
    box_id = lax.broadcasted_iota(jnp.int32, (boxes, kids), 0)
    even = jnp.where(box_id == slot, 1.0, 0.0)
    odd = jnp.where(box_id == slot + 1, 1.0, 0.0)
    filled = even + odd
    offset = jnp.sum(filled * off_ref[...], axis=1, keepdims=True)
    offset = offset + jnp.sum(filled, axis=1, keepdims=True) - 1.0
    outbox[:, pl.ds(0, TAG)] = jnp.broadcast_to(offset, (boxes, TAG))
    choose = jnp.concatenate([even, odd], axis=1).astype(BF16)

    def pack(m):
        lo = pl.multiple_of(m * 2 * HC, HC)
        both = jnp.concatenate(
            [child_ref[:, pl.ds(lo, HC)], child_ref[:, pl.ds(pl.multiple_of(lo + HC, HC), HC)]],
            axis=0,
        )
        outbox[:, pl.ds(pl.multiple_of(TAG + m * HC, TAG), HC)] = place(choose, both)

    nblk = total_cols // (2 * HC)
    bands = [
        (0, TAG + HC),
        (TAG + HC, 3 * HC),
        (TAG + 4 * HC, (nblk - 4) * HC),
    ]

    def mail(band, d):
        peer = lax.rem(r + d, count)
        cols = pl.ds(*bands[band])
        return pltpu.make_async_remote_copy(
            src_ref=outbox.at[pl.ds(mult8(8 * peer), 8), cols],
            dst_ref=inbox.at[pl.ds(mult8(8 * r), 8), cols],
            send_sem=box_send.at[band, d],
            recv_sem=box_recv.at[band, d],
            device_id={"row": peer},
            device_id_type=MESH,
        )

    def over_peers(action):
        def body(d, carry):
            action(d)
            return carry

        lax.fori_loop(1, count, body, 0)

    def post(band):
        over_peers(lambda d: mail(band, d).start())
        mine = pl.ds(mult8(8 * r), 8)
        cols = pl.ds(*bands[band])
        inbox[mine, cols] = outbox[mine, cols]

    def collect(band):
        over_peers(lambda d: mail(band, d).wait_recv())

    pack(0)
    pl.semaphore_wait(barrier, count - 1 + 2)
    post(0)
    for m in range(1, 4):
        pack(m)
    post(1)
    for m in range(4, nblk):
        pack(m)
    post(2)

    collect(0)
    place_at = jnp.transpose(inbox[:, pl.ds(0, TAG)])[0:1, :]
    row_id = lax.broadcasted_iota(jnp.int32, (rows, boxes), 0).astype(F32)
    parity = lax.rem(lax.broadcasted_iota(jnp.int32, (rows, boxes), 1), 2)
    hit = row_id == place_at
    for h in range(2):
        onehot[h] = jnp.where(jnp.logical_and(hit, parity == h), 1.0, 0.0).astype(BF16)

    def assemble(m):
        value = inbox[:, pl.ds(pl.multiple_of(TAG + m * HC, TAG), HC)]
        high, mid, low = split3(value)
        for h in range(2):
            hot = onehot[h]
            cols = pl.ds(pl.multiple_of((2 * m + h) * HC, HC), HC)
            added = jnp.dot(hot, high, preferred_element_type=F32) + (
                jnp.dot(hot, mid, preferred_element_type=F32)
                + jnp.dot(hot, low, preferred_element_type=F32)
            )
            w_ref[:, cols] = w_ref[:, cols] + added

    load.wait()
    assemble(0)

    nz = rows // 2 // ZROWS

    def pass_on(way, q):
        start = (q if way == 0 else nz + q) * ZROWS
        piece = a1_ref.at[pl.ds(start, ZROWS), :]
        return pltpu.make_async_remote_copy(
            src_ref=piece,
            dst_ref=piece,
            send_sem=z_send.at[way, q],
            recv_sem=z_recv.at[way, q],
            device_id={"col": z_up if way == 0 else z_dn},
            device_id_type=MESH,
        )

    @pl.when(z == 0)
    def _():
        a1_ref[...] = w_ref[:, pl.ds(0, WIDE)]
        for q in range(nz):
            for way in range(2):
                pass_on(way, q).start()

    for near in range(2):
        @pl.when(z == (1 if near == 0 else deep - 1))
        def _():
            for q in range(nz):
                pass_on(near, q).wait_recv()
                pass_on(near, q).start()
            for q in range(nz):
                pass_on(1 - near, q).wait_recv()

    @pl.when(z == 2)
    def _():
        for q in range(nz):
            for way in range(2):
                pass_on(way, q).wait_recv()
                pass_on(way, q).start()

    a1_save = pltpu.make_async_copy(a1_ref, a1_out, local_sem.at[1])
    a1_save.start()
    a1t = jnp.transpose(a1_ref[...])
    hi, lo = split(a1t)
    ah[...] = hi
    al[...] = lo
    p_ref[:, pl.ds(0, WIDE)] = product(a1t, a1_ref[...])

    a_up, a_dn, a_op = lax.rem(a + 1, SIDE), lax.rem(a + 3, SIDE), lax.rem(a + 2, SIDE)
    b_up, b_dn, b_op = lax.rem(b + 1, SIDE), lax.rem(b + 3, SIDE), lax.rem(b + 2, SIDE)
    dev = {
        "p": r + 1 - 2 * core,
        "a+": at(a_up, b),
        "a-": at(a_dn, b),
        "ao": at(a_op, b),
        "b+": at(a, b_up),
        "b-": at(a, b_dn),
        "bo": at(a, b_op),
    }
    chunks = [(0, WIDE)] + [(WIDE + i * CW, CW) for i in range(total_cols // CW)]
    n = len(chunks)
    started = {}
    saves = []

    def send(c, slot, src, dst, where):
        copy = pltpu.make_async_remote_copy(
            src_ref=src,
            dst_ref=dst,
            send_sem=send_sem.at[c, slot],
            recv_sem=recv_sem.at[c, slot],
            device_id={"row": dev[where]},
            device_id_type=MESH,
        )
        copy.start()
        started[(c, slot)] = copy

    def got(c, *slots):
        for slot in slots:
            started[(c, slot)].wait_recv()

    own = HALF * core

    def shard(i, half=0):
        return mult8(own + SHARD * i + half * (SHARD // 2))

    def sub(i, half=0):
        return mult8(own + SHARD * a + SUB * i + half * (SUB // 2))

    s32, s8 = SHARD // 2, SUB // 2

    def fill(c):
        if c == 2:
            collect(1)
            for m in range(1, 4):
                assemble(m)
        if c == 5:
            collect(2)
            for m in range(4, nblk):
                assemble(m)
            save = pltpu.make_async_copy(w_ref, w_out, local_sem.at[2])
            save.start()
            saves.append(save)
        for i in range(CW // 256):
            off = (c - 1) * CW + i * 256
            wh, wl = split(w_ref[:, pl.ds(off, 256)])
            p_ref[:, pl.ds(off + WIDE, 256)] = dot3(ah[...], al[...], wh, wl)

    def tools(c):
        cols = pl.ds(*chunks[c])

        def part(row, size):
            return p_ref.at[pl.ds(row, size), cols]

        def full(row, size):
            return f_ref.at[pl.ds(row, size), cols]

        def add(row, size, *sources, into=p_ref):
            span = pl.ds(row, size)
            value = p_ref[span, cols]
            for source in sources:
                value = value + source[...]
            into[span, cols] = value

        def one(i, size=s32):
            return r1.at[pl.ds(i * size, size), cols]

        def two(i, size=s8):
            return r2.at[pl.ds(i * size, size), cols]

        return cols, part, full, add, one, two

    def phase_gram(p):
        c = 0
        cols, part, full, add, one, two = tools(c)
        if p == 0:
            send(c, 0, part(mult8(HALF * other), HALF), r0.at[:, cols], "p")
        elif p == 1:
            got(c, 0)
            add(mult8(own), HALF, r0.at[:, cols])
            send(c, 1, part(shard(a_op), SHARD), one(0, SHARD), "ao")
            send(c, 2, part(shard(a_up), SHARD), one(1, SHARD), "a+")
            send(c, 3, part(shard(a_dn), SHARD), one(2, SHARD), "a-")
        elif p == 2:
            got(c, 2, 3, 1)
            add(shard(a), SHARD, one(0, SHARD), one(1, SHARD), one(2, SHARD))
            send(c, 4, part(sub(b_op), SUB), two(0, SUB), "bo")
            send(c, 5, part(sub(b_up), SUB), two(1, SUB), "b+")
            send(c, 6, part(sub(b_dn), SUB), two(2, SUB), "b-")
        elif p == 3:
            got(c, 5, 6, 4)
            add(sub(b), SUB, two(0, SUB), two(1, SUB), two(2, SUB), into=f_ref)
            for slot, where in ((7, "bo"), (8, "b+"), (9, "b-")):
                send(c, slot, full(sub(b), SUB), full(sub(b), SUB), where)
        elif p == 4:
            got(c, 8, 9, 7)
            for slot, where in ((10, "ao"), (11, "a+"), (12, "a-")):
                send(c, slot, full(shard(a), SHARD), full(shard(a), SHARD), where)
        elif p == 5:
            got(c, 11, 12, 10)
            send(c, 13, full(mult8(own), HALF), full(mult8(own), HALF), "p")
        elif p == 6:
            got(c, 13)

    def phase(c, p):
        cols, part, full, add, one, two = tools(c)
        if p == 0:
            fill(c)
            send(c, 0, part(mult8(HALF * other), HALF), r0.at[:, cols], "p")
        elif p == 1:
            got(c, 0)
            add(mult8(own), HALF, r0.at[:, cols])
            send(c, 1, part(shard(a_op, 0), s32), one(0), "a+")
            send(c, 2, part(shard(a_op, 1), s32), one(1), "a-")
            send(c, 3, part(shard(a_up, 1), s32), one(2), "a+")
            send(c, 4, part(shard(a_dn, 0), s32), one(3), "a-")
        elif p == 2:
            got(c, 1)
            add(shard(a_up, 0), s32, one(0))
            send(c, 5, part(shard(a_up, 0), s32), one(4), "a+")
            got(c, 2)
            add(shard(a_dn, 1), s32, one(1))
            send(c, 6, part(shard(a_dn, 1), s32), one(5), "a-")
        elif p == 3:
            got(c, 3, 4, 5, 6)
            add(shard(a, 0), s32, one(3), one(4))
            add(shard(a, 1), s32, one(2), one(5))
            send(c, 7, part(sub(b_op, 0), s8), two(0), "b+")
            send(c, 8, part(sub(b_op, 1), s8), two(1), "b-")
            send(c, 9, part(sub(b_up, 1), s8), two(2), "b+")
            send(c, 10, part(sub(b_dn, 0), s8), two(3), "b-")
        elif p == 4:
            got(c, 7)
            add(sub(b_up, 0), s8, two(0))
            send(c, 11, part(sub(b_up, 0), s8), two(4), "b+")
            got(c, 8)
            add(sub(b_dn, 1), s8, two(1))
            send(c, 12, part(sub(b_dn, 1), s8), two(5), "b-")
        elif p == 5:
            got(c, 9, 10, 11, 12)
            add(sub(b, 0), s8, two(3), two(4), into=f_ref)
            add(sub(b, 1), s8, two(2), two(5), into=f_ref)
            send(c, 13, full(sub(b), SUB), full(sub(b), SUB), "b+")
            send(c, 14, full(sub(b), SUB), full(sub(b), SUB), "b-")
        elif p == 6:
            got(c, 13)
            send(c, 15, full(sub(b_dn, 0), s8), full(sub(b_dn, 0), s8), "b+")
            got(c, 14)
            send(c, 16, full(sub(b_up, 1), s8), full(sub(b_up, 1), s8), "b-")
        elif p == 7:
            got(c, 15, 16)
            send(c, 17, full(shard(a), SHARD), full(shard(a), SHARD), "a+")
            send(c, 18, full(shard(a), SHARD), full(shard(a), SHARD), "a-")
        elif p == 8:
            got(c, 17)
            send(c, 19, full(shard(a_dn, 0), s32), full(shard(a_dn, 0), s32), "a+")
            got(c, 18)
            send(c, 20, full(shard(a_up, 1), s32), full(shard(a_up, 1), s32), "a-")
        elif p == 9:
            got(c, 19, 20)
            send(c, 21, full(mult8(own), HALF), full(mult8(own), HALF), "p")
        elif p == 10:
            got(c, 21)
            save = pltpu.make_async_copy(
                f_ref.at[:, cols],
                f_out.at[:, pl.ds((c - 1) * CW, CW)],
                local_sem.at[2 + c],
            )
            save.start()
            saves.append(save)

    def chol_begin(k):
        if k == 0:
            g_ref[...] = f_ref[:, pl.ds(0, WIDE)]
            linv_ref[...] = jnp.zeros_like(linv_ref)
        d = pl.ds(k * PB, PB)
        dblk[...] = g_ref[d, d]
        xblk[...] = jnp.where(
            lax.broadcasted_iota(jnp.int32, (PB, PB), 0)
            == lax.broadcasted_iota(jnp.int32, (PB, PB), 1),
            1.0,
            0.0,
        ).astype(F32)

    def chol_end(k):
        d = pl.ds(k * PB, PB)
        x = xblk[...]
        if k:
            left = pl.ds(0, k * PB)
            linv_ref[d, left] = -product(x, product(g_ref[d, left], linv_ref[left, left]))
        linv_ref[d, d] = x
        if k < PANELS - 1:
            rest = pl.ds((k + 1) * PB, (PANELS - 1 - k) * PB)
            below = tdot(g_ref[rest, d], x)
            g_ref[rest, d] = below
            g_ref[rest, rest] = g_ref[rest, rest] - tdot(below, below)

    pieces = []
    for k in range(PANELS):
        for q in range(PIECES):
            pieces.append((k, q))

    def piece(k, q):
        if q == 0:
            chol_begin(k)
        chol_steps(dblk, xblk, q * (PB // PIECES), (q + 1) * (PB // PIECES))
        if q == PIECES - 1:
            chol_end(k)

    steps = [(GRAM_TAU[p], 0, p) for p in range(7)]
    steps += [(2 * p + c, c, p) for c in range(1, n) for p in range(11)]
    before = None
    ready = False
    for tau, c, p in sorted(steps):
        if ready and tau != before and pieces:
            piece(*pieces.pop(0))
        before = tau
        if c == 0:
            phase_gram(p)
        else:
            phase(c, p)
        ready = ready or (c, p) == (0, 6)
    for rest in pieces:
        piece(*rest)

    for copy in started.values():
        copy.wait_send()
    for band in range(len(bands)):
        over_peers(lambda d: mail(band, d).wait_send())
    for way in range(2):
        end = deep - 1 if way == 0 else 1

        @pl.when(z != end)
        def _():
            for q in range(nz):
                pass_on(way, q).wait_send()

    a1_save.wait()
    for save in saves:
        save.wait()


def all_reduced(front, child, owner, offset):
    rows, cols = front.shape
    kids = child.shape[0]
    count, deep = lax.axis_size("row"), lax.axis_size("col")
    wide = cols + WIDE
    n = 1 + cols // CW
    vm = pl.BlockSpec(memory_space=pltpu.VMEM)
    hbm = pl.BlockSpec(memory_space=pl.ANY)
    dma = pltpu.SemaphoreType.DMA
    box = TAG + cols // 2
    return pl.pallas_call(
        main_kernel,
        out_shape=(
            jax.ShapeDtypeStruct((rows, cols), F32),
            jax.ShapeDtypeStruct((WIDE, cols), F32),
            jax.ShapeDtypeStruct((rows, WIDE), F32),
            jax.ShapeDtypeStruct((WIDE, WIDE), F32),
        ),
        in_specs=[vm, vm, vm, vm, hbm],
        out_specs=(hbm, hbm, hbm, vm),
        scratch_shapes=[
            pltpu.VMEM((rows, cols), F32),
            pltpu.VMEM((WIDE, wide), F32),
            pltpu.VMEM((WIDE, wide), F32),
            pltpu.VMEM((rows, WIDE), F32),
            pltpu.VMEM((WIDE, rows), BF16),
            pltpu.VMEM((WIDE, rows), BF16),
            pltpu.VMEM((HALF, wide), F32),
            pltpu.VMEM((6 * SHARD // 2, wide), F32),
            pltpu.VMEM((6 * SUB // 2, wide), F32),
            pltpu.VMEM((WIDE, WIDE), F32),
            pltpu.VMEM((PB, PB), F32),
            pltpu.VMEM((PB, PB), F32),
            pltpu.VMEM((8 * count, box), F32),
            pltpu.VMEM((8 * count, box), F32),
            pltpu.VMEM((2, rows, 8 * count), BF16),
            dma((n, COPIES)),
            dma((n, COPIES)),
            dma((3, count)),
            dma((3, count)),
            dma((2, rows // 2 // ZROWS)),
            dma((2, rows // 2 // ZROWS)),
            dma((2 + n,)),
        ],
        compiler_params=pltpu.CompilerParams(
            collective_id=0, has_side_effects=True, vmem_limit_bytes=63 * 1024 * 1024
        ),
        name="assemble_and_reduce",
    )(
        child,
        owner,
        owner.reshape(1, kids),
        offset.reshape(1, kids).astype(F32),
        front,
    )


def tail_kernel(scale, a1_ref, linv_ref, s_ref, w_ref, u_ref, o_ref, q_ref, lh, ll, qh, ql):
    @pl.when(pl.program_id(0) == 0)
    def _():
        linv = linv_ref[...]
        hi, lo = split(linv)
        lh[...] = hi
        ll[...] = lo
        basis = tdot(a1_ref[...], linv)
        q_ref[...] = basis * scale
        hi, lo = split(basis)
        qh[...] = hi
        ql[...] = lo

    sh, sl = split(s_ref[...])
    u = dot3(lh[...], ll[...], sh, sl)
    u_ref[...] = u
    uh, ul = split(u)
    o_ref[...] = w_ref[...] - dot3(qh[...], ql[...], uh, ul)


def tail(a1, linv, sums, w, scale):
    rows, cols = w.shape
    tc = 512
    whole = lambda shape: pl.BlockSpec(shape, lambda i: (0, 0))
    return pl.pallas_call(
        functools.partial(tail_kernel, scale),
        grid=(cols // tc,),
        out_shape=(
            jax.ShapeDtypeStruct((WIDE, cols), F32),
            jax.ShapeDtypeStruct((rows, cols), F32),
            jax.ShapeDtypeStruct((rows, WIDE), F32),
        ),
        in_specs=[
            whole((rows, WIDE)),
            whole((WIDE, WIDE)),
            pl.BlockSpec((WIDE, tc), lambda i: (0, i)),
            pl.BlockSpec((rows, tc), lambda i: (0, i)),
        ],
        out_specs=(
            pl.BlockSpec((WIDE, tc), lambda i: (0, i)),
            pl.BlockSpec((rows, tc), lambda i: (0, i)),
            whole((rows, WIDE)),
        ),
        scratch_shapes=[
            pltpu.VMEM((WIDE, WIDE), BF16),
            pltpu.VMEM((WIDE, WIDE), BF16),
            pltpu.VMEM((rows, WIDE), BF16),
            pltpu.VMEM((rows, WIDE), BF16),
        ],
        compiler_params=pltpu.CompilerParams(vmem_limit_bytes=40 * 1024 * 1024),
        name="project_out",
    )(a1, linv, sums, w)


def on_device(front_matrix, child_rows, child_owner, child_offset):
    total_rows = front_matrix.shape[0] * lax.axis_size("row")
    current, sums, panel, linv = all_reduced(front_matrix, child_rows, child_owner, child_offset)
    return tail(panel, linv, sums, current, math.sqrt(total_rows))


def solution(mesh):
    placed = (P("row", "col"), P("row", "col"), P("row", None), P("row", None))
    return jax.shard_map(
        on_device,
        mesh=mesh,
        in_specs=placed,
        out_specs=(P(None, "col"), P("row", "col"), P("row", None)),
        check_vma=False,
    )
```

```python
import functools
import math

import jax
import jax.numpy as jnp
from jax import lax
from jax.experimental import pallas as pl
from jax.experimental.pallas import tpu as pltpu
from jax.sharding import PartitionSpec as P

PB = 128
PANELS = 4
WIDE = PB * PANELS
MESH = pl.DeviceIdType.MESH
F32 = jnp.float32
BF16 = jnp.bfloat16
SIDE = 4
HALF = WIDE // 2
SHARD = HALF // SIDE
SUB = SHARD // SIDE
CW = 512
HC = 256
TAG = 128
GROUP = 4
GRAM_TAU = (-2, -1, 2, 3, 4, 5, 6)
PIECES = 4
COPIES = 22
ZROWS = 32
BROWS = 64


def product(left_op, right_op):
    return jnp.dot(
        left_op, right_op, precision=lax.Precision.HIGHEST, preferred_element_type=F32
    )


def split(value):
    high = value.astype(BF16)
    return high, (value - high.astype(F32)).astype(BF16)


def split3(value):
    high = value.astype(BF16)
    rest = value - high.astype(F32)
    mid = rest.astype(BF16)
    return high, mid, (rest - mid.astype(F32)).astype(BF16)


def place(onehot, value):
    high, mid, low = split3(value)

    def one(part):
        return jnp.dot(onehot, part, preferred_element_type=F32)

    return one(high) + (one(mid) + one(low))


def dot3(lh, ll, rh, rl):
    def one(a, b):
        return jnp.dot(a, b, preferred_element_type=F32)

    return one(lh, rh) + (one(lh, rl) + one(ll, rh))


def chol_steps(dblk, xblk, start, stop):
    lane = lax.broadcasted_iota(jnp.int32, (PB, PB), 1)
    lane1 = lax.broadcasted_iota(jnp.int32, (1, PB), 1)
    sub = lax.broadcasted_iota(jnp.int32, (PB, PB), 0)

    def step(i, carry):
        j = i * GROUP
        a, x = dblk[...], xblk[...]
        span = range(GROUP)
        rows = [dblk[pl.ds(j + q, 1), :] for q in span]
        xrows = [xblk[pl.ds(j + q, 1), :] for q in span]
        cols = [
            jnp.sum(jnp.where(lane == j + q, a, 0.0), axis=1, keepdims=True) for q in span
        ]
        m = {
            (p, q): jnp.sum(jnp.where(lane1 == j + q, rows[p], 0.0), axis=1, keepdims=True)
            for p in span
            for q in range(p, GROUP)
        }
        invs = []
        for p in span:
            inv = lax.rsqrt(m[p, p])
            inv2 = inv * inv
            invs.append(inv)
            for q in range(p + 1, GROUP):
                f = m[p, q] * inv2
                rows[q] = rows[q] - f * rows[p]
                xrows[q] = xrows[q] - f * xrows[p]
                cols[q] = cols[q] - f * cols[p]
                for r in range(q, GROUP):
                    m[q, r] = m[q, r] - f * m[p, r]
            cols[p] = cols[p] * inv2
        below = sub > j + GROUP - 1
        na, nx = a, x
        for p in span:
            na = na - cols[p] * rows[p]
            nx = nx - cols[p] * xrows[p]
        nx = jnp.where(below, nx, x)
        for p in span:
            nx = jnp.where(sub == j + p, xrows[p] * invs[p], nx)
        dblk[...] = jnp.where(below, na, a)
        xblk[...] = nx
        return carry

    lax.fori_loop(start // GROUP, stop // GROUP, step, 0)


def tdot(a, b):
    return lax.dot_general(
        a, b, (((1,), (1,)), ((), ())), precision=lax.Precision.HIGHEST, preferred_element_type=F32
    )


def main_kernel(
    child_ref, ocol_ref, orow_ref, off_ref, front_ref,
    w_out, f_out, a1_out, linv_ref,
    w_ref, f_ref, p_ref, a1_ref, a1_full, ah, al, r0, r1, r2, g_ref, dblk, xblk,
    outbox, inbox, zbox, onehot, lh, ll, u_ref,
    send_sem, recv_sem, box_send, box_recv, z_send, z_recv, local_sem,
):
    count = lax.axis_size("row")
    deep = lax.axis_size("col")
    r = lax.axis_index("row")
    z = lax.axis_index("col")
    core = lax.rem(r, 2)
    yy = lax.rem(r // 2, SIDE)
    xx = r // (2 * SIDE)
    other = 1 - core
    a = other * xx + core * yy
    b = core * xx + other * yy
    rows, total_cols = w_ref.shape
    kids = child_ref.shape[0]

    def mult8(v, m=8):
        return pl.multiple_of(v, m)

    def at(first, second):
        px = other * first + core * second
        py = core * first + other * second
        return (px * SIDE + py) * 2 + core

    first = pltpu.make_async_copy(front_ref.at[:, pl.ds(0, WIDE)], a1_ref, local_sem.at[1])

    @pl.when(z == 0)
    def _():
        first.start()

    load = pltpu.make_async_copy(front_ref, w_ref, local_sem.at[0])
    load.start()

    barrier = pltpu.get_barrier_semaphore()

    def greet(d, carry):
        pl.semaphore_signal(
            barrier, inc=1, device_id={"row": lax.rem(r + d, count)}, device_id_type=MESH
        )
        return carry

    lax.fori_loop(1, count, greet, 0)
    z_up, z_dn = lax.rem(z + 1, deep), lax.rem(z + deep - 1, deep)
    for peer in (z_up, z_dn):
        pl.semaphore_signal(barrier, inc=1, device_id={"col": peer}, device_id_type=MESH)

    orow = orow_ref[...]
    earlier = lax.broadcasted_iota(jnp.int32, (kids, kids), 0) < lax.broadcasted_iota(
        jnp.int32, (kids, kids), 1
    )
    same = jnp.logical_and(ocol_ref[...] == orow, earlier)
    rank = jnp.sum(jnp.where(same, 1.0, 0.0), axis=0, keepdims=True).astype(jnp.int32)
    slot = orow * 8 + rank * 2
    boxes = 8 * count
    box_id = lax.broadcasted_iota(jnp.int32, (boxes, kids), 0)
    even = jnp.where(box_id == slot, 1.0, 0.0)
    odd = jnp.where(box_id == slot + 1, 1.0, 0.0)
    filled = even + odd
    offset = jnp.sum(filled * off_ref[...], axis=1, keepdims=True)
    offset = offset + jnp.sum(filled, axis=1, keepdims=True) - 1.0
    outbox[:, pl.ds(0, TAG)] = jnp.broadcast_to(offset, (boxes, TAG))
    choose = jnp.concatenate([even, odd], axis=1).astype(BF16)

    def pack(m):
        lo = pl.multiple_of(m * 2 * HC, HC)
        both = jnp.concatenate(
            [child_ref[:, pl.ds(lo, HC)], child_ref[:, pl.ds(pl.multiple_of(lo + HC, HC), HC)]],
            axis=0,
        )
        outbox[:, pl.ds(pl.multiple_of(TAG + m * HC, TAG), HC)] = place(choose, both)

    nblk = total_cols // (2 * HC)
    bands = [
        (0, TAG + HC),
        (TAG + HC, 3 * HC),
        (TAG + 4 * HC, (nblk - 4) * HC),
    ]

    peers = [
        (dx, dy, dc)
        for dc in (1, 0)
        for dy in range(SIDE)
        for dx in (1, 3, 2, 0)
        if (dx, dy, dc) != (0, 0, 0)
    ]
    turn = 1 - 2 * core

    def mail(band, k):
        dx, dy, dc = peers[k]
        px = lax.rem(xx + turn * dx + SIDE, SIDE)
        py = lax.rem(yy + turn * dy + SIDE, SIDE)
        peer = (px * SIDE + py) * 2 + lax.rem(core + dc, 2)
        cols = pl.ds(*bands[band])
        return pltpu.make_async_remote_copy(
            src_ref=outbox.at[pl.ds(mult8(8 * peer), 8), cols],
            dst_ref=inbox.at[pl.ds(mult8(8 * r), 8), cols],
            send_sem=box_send.at[band, k],
            recv_sem=box_recv.at[band, k],
            device_id={"row": peer},
            device_id_type=MESH,
        )

    def over_peers(action):
        for k in range(len(peers)):
            action(k)

    def post(band):
        over_peers(lambda k: mail(band, k).start())
        mine = pl.ds(mult8(8 * r), 8)
        cols = pl.ds(*bands[band])
        inbox[mine, cols] = outbox[mine, cols]

    def collect(band):
        over_peers(lambda k: mail(band, k).wait_recv())

    na, nb = rows // 2 // ZROWS, boxes // 2 // BROWS

    def pass_on(way, q):
        if q < na:
            piece = a1_ref.at[pl.ds((way * na + q) * ZROWS, ZROWS), :]
        else:
            piece = zbox.at[pl.ds((way * nb + q - na) * BROWS, BROWS), :]
        return pltpu.make_async_remote_copy(
            src_ref=piece,
            dst_ref=piece,
            send_sem=z_send.at[way, q],
            recv_sem=z_recv.at[way, q],
            device_id={"col": z_up if way == 0 else z_dn},
            device_id_type=MESH,
        )

    def source(span):
        @pl.when(z == 0)
        def _():
            for q in span:
                for way in range(2):
                    pass_on(way, q).start()

    def near(span):
        for way in range(2):
            @pl.when(z == (1 if way == 0 else deep - 1))
            def _():
                for q in span:
                    pass_on(way, q).wait_recv()
                    pass_on(way, q).start()

        @pl.when(z == 2)
        def _():
            for q in span:
                for way in range(2):
                    pass_on(way, q).wait_recv()
                    pass_on(way, q).start()

    def far(span):
        for way in range(2):
            @pl.when(z == (1 if way == 1 else deep - 1))
            def _():
                for q in span:
                    pass_on(way, q).wait_recv()

    pack(0)

    @pl.when(z == 0)
    def _():
        first.wait()

    pl.semaphore_wait(barrier, count - 1 + 2)
    post(0)
    source(range(na))
    for m in range(1, 4):
        pack(m)
    post(1)
    for m in range(4, nblk):
        pack(m)
    post(2)
    near(range(na))

    collect(0)

    @pl.when(z == 0)
    def _():
        zbox[...] = inbox[:, pl.ds(TAG, HC)]

    source(range(na, na + nb))
    place_at = jnp.transpose(inbox[:, pl.ds(0, TAG)])[0:1, :]
    row_id = lax.broadcasted_iota(jnp.int32, (rows, boxes), 0).astype(F32)
    parity = lax.rem(lax.broadcasted_iota(jnp.int32, (rows, boxes), 1), 2)
    hit = row_id == place_at
    for h in range(2):
        onehot[h] = jnp.where(jnp.logical_and(hit, parity == h), 1.0, 0.0).astype(BF16)

    def assemble(m):
        value = inbox[:, pl.ds(pl.multiple_of(TAG + m * HC, TAG), HC)]
        high, mid, low = split3(value)
        for h in range(2):
            hot = onehot[h]
            cols = pl.ds(pl.multiple_of((2 * m + h) * HC, HC), HC)
            added = jnp.dot(hot, high, preferred_element_type=F32) + (
                jnp.dot(hot, mid, preferred_element_type=F32)
                + jnp.dot(hot, low, preferred_element_type=F32)
            )
            w_ref[:, cols] = w_ref[:, cols] + added

    near(range(na, na + nb))
    load.wait()
    assemble(0)
    far(range(na + nb))
    value = zbox[...]
    for h in range(2):
        cols = pl.ds(h * HC, HC)
        a1_full[:, cols] = a1_ref[:, cols] + place(onehot[h], value)

    a1_save = pltpu.make_async_copy(a1_full, a1_out, local_sem.at[1])
    a1_save.start()
    a1t = jnp.transpose(a1_full[...])
    hi, lo = split(a1t)
    ah[...] = hi
    al[...] = lo
    p_ref[:, pl.ds(0, WIDE)] = product(a1t, a1_full[...])

    a_up, a_dn, a_op = lax.rem(a + 1, SIDE), lax.rem(a + 3, SIDE), lax.rem(a + 2, SIDE)
    b_up, b_dn, b_op = lax.rem(b + 1, SIDE), lax.rem(b + 3, SIDE), lax.rem(b + 2, SIDE)
    dev = {
        "p": r + 1 - 2 * core,
        "a+": at(a_up, b),
        "a-": at(a_dn, b),
        "ao": at(a_op, b),
        "b+": at(a, b_up),
        "b-": at(a, b_dn),
        "bo": at(a, b_op),
    }
    chunks = [(0, WIDE)] + [(WIDE + i * CW, CW) for i in range(total_cols // CW)]
    n = len(chunks)
    started = {}
    saves = []

    def send(c, slot, src, dst, where):
        copy = pltpu.make_async_remote_copy(
            src_ref=src,
            dst_ref=dst,
            send_sem=send_sem.at[c, slot],
            recv_sem=recv_sem.at[c, slot],
            device_id={"row": dev[where]},
            device_id_type=MESH,
        )
        copy.start()
        started[(c, slot)] = copy

    def got(c, *slots):
        for slot in slots:
            started[(c, slot)].wait_recv()

    own = HALF * core

    def shard(i, half=0):
        return mult8(own + SHARD * i + half * (SHARD // 2))

    def sub(i, half=0):
        return mult8(own + SHARD * a + SUB * i + half * (SUB // 2))

    s32, s8 = SHARD // 2, SUB // 2

    def fill(c):
        if c == 2:
            collect(1)
            for m in range(1, 4):
                assemble(m)
        if c == 5:
            collect(2)
            for m in range(4, nblk):
                assemble(m)
            save = pltpu.make_async_copy(w_ref, w_out, local_sem.at[2])
            save.start()
            saves.append(save)
        for i in range(CW // 256):
            off = (c - 1) * CW + i * 256
            wh, wl = split(w_ref[:, pl.ds(off, 256)])
            p_ref[:, pl.ds(off + WIDE, 256)] = dot3(ah[...], al[...], wh, wl)

    def tools(c):
        cols = pl.ds(*chunks[c])

        def part(row, size):
            return p_ref.at[pl.ds(row, size), cols]

        def full(row, size):
            return f_ref.at[pl.ds(row, size), cols]

        def add(row, size, *sources, into=p_ref):
            span = pl.ds(row, size)
            value = p_ref[span, cols]
            for source in sources:
                value = value + source[...]
            into[span, cols] = value

        def one(i, size=s32):
            return r1.at[pl.ds(i * size, size), cols]

        def two(i, size=s8):
            return r2.at[pl.ds(i * size, size), cols]

        return cols, part, full, add, one, two

    def phase_gram(p):
        c = 0
        cols, part, full, add, one, two = tools(c)
        if p == 0:
            send(c, 0, part(mult8(HALF * other), HALF), r0.at[:, cols], "p")
        elif p == 1:
            got(c, 0)
            add(mult8(own), HALF, r0.at[:, cols])
            send(c, 1, part(shard(a_op), SHARD), one(0, SHARD), "ao")
            send(c, 2, part(shard(a_up), SHARD), one(1, SHARD), "a+")
            send(c, 3, part(shard(a_dn), SHARD), one(2, SHARD), "a-")
        elif p == 2:
            got(c, 2, 3, 1)
            add(shard(a), SHARD, one(0, SHARD), one(1, SHARD), one(2, SHARD))
            send(c, 4, part(sub(b_op), SUB), two(0, SUB), "bo")
            send(c, 5, part(sub(b_up), SUB), two(1, SUB), "b+")
            send(c, 6, part(sub(b_dn), SUB), two(2, SUB), "b-")
        elif p == 3:
            got(c, 5, 6, 4)
            add(sub(b), SUB, two(0, SUB), two(1, SUB), two(2, SUB), into=f_ref)
            for slot, where in ((7, "bo"), (8, "b+"), (9, "b-")):
                send(c, slot, full(sub(b), SUB), full(sub(b), SUB), where)
        elif p == 4:
            got(c, 8, 9, 7)
            for slot, where in ((10, "ao"), (11, "a+"), (12, "a-")):
                send(c, slot, full(shard(a), SHARD), full(shard(a), SHARD), where)
        elif p == 5:
            got(c, 11, 12, 10)
            send(c, 13, full(mult8(own), HALF), full(mult8(own), HALF), "p")
        elif p == 6:
            got(c, 13)

    def phase(c, p):
        cols, part, full, add, one, two = tools(c)
        if p == 0:
            fill(c)
            send(c, 0, part(mult8(HALF * other), HALF), r0.at[:, cols], "p")
        elif p == 1:
            got(c, 0)
            add(mult8(own), HALF, r0.at[:, cols])
            send(c, 1, part(shard(a_op, 0), s32), one(0), "a+")
            send(c, 2, part(shard(a_op, 1), s32), one(1), "a-")
            send(c, 3, part(shard(a_up, 1), s32), one(2), "a+")
            send(c, 4, part(shard(a_dn, 0), s32), one(3), "a-")
        elif p == 2:
            got(c, 1)
            add(shard(a_up, 0), s32, one(0))
            send(c, 5, part(shard(a_up, 0), s32), one(4), "a+")
            got(c, 2)
            add(shard(a_dn, 1), s32, one(1))
            send(c, 6, part(shard(a_dn, 1), s32), one(5), "a-")
        elif p == 3:
            got(c, 3, 4, 5, 6)
            add(shard(a, 0), s32, one(3), one(4))
            add(shard(a, 1), s32, one(2), one(5))
            send(c, 7, part(sub(b_op, 0), s8), two(0), "b+")
            send(c, 8, part(sub(b_op, 1), s8), two(1), "b-")
            send(c, 9, part(sub(b_up, 1), s8), two(2), "b+")
            send(c, 10, part(sub(b_dn, 0), s8), two(3), "b-")
        elif p == 4:
            got(c, 7)
            add(sub(b_up, 0), s8, two(0))
            send(c, 11, part(sub(b_up, 0), s8), two(4), "b+")
            got(c, 8)
            add(sub(b_dn, 1), s8, two(1))
            send(c, 12, part(sub(b_dn, 1), s8), two(5), "b-")
        elif p == 5:
            got(c, 9, 10, 11, 12)
            add(sub(b, 0), s8, two(3), two(4), into=f_ref)
            add(sub(b, 1), s8, two(2), two(5), into=f_ref)
            send(c, 13, full(sub(b), SUB), full(sub(b), SUB), "b+")
            send(c, 14, full(sub(b), SUB), full(sub(b), SUB), "b-")
        elif p == 6:
            got(c, 13)
            send(c, 15, full(sub(b_dn, 0), s8), full(sub(b_dn, 0), s8), "b+")
            got(c, 14)
            send(c, 16, full(sub(b_up, 1), s8), full(sub(b_up, 1), s8), "b-")
        elif p == 7:
            got(c, 15, 16)
            send(c, 17, full(shard(a), SHARD), full(shard(a), SHARD), "a+")
            send(c, 18, full(shard(a), SHARD), full(shard(a), SHARD), "a-")
        elif p == 8:
            got(c, 17)
            send(c, 19, full(shard(a_dn, 0), s32), full(shard(a_dn, 0), s32), "a+")
            got(c, 18)
            send(c, 20, full(shard(a_up, 1), s32), full(shard(a_up, 1), s32), "a-")
        elif p == 9:
            got(c, 19, 20)
            send(c, 21, full(mult8(own), HALF), full(mult8(own), HALF), "p")
        elif p == 10:
            got(c, 21)
            summed.append(c)

    def chol_begin(k):
        if k == 0:
            g_ref[...] = f_ref[:, pl.ds(0, WIDE)]
            linv_ref[...] = jnp.zeros_like(linv_ref)
        d = pl.ds(k * PB, PB)
        dblk[...] = g_ref[d, d]
        xblk[...] = jnp.where(
            lax.broadcasted_iota(jnp.int32, (PB, PB), 0)
            == lax.broadcasted_iota(jnp.int32, (PB, PB), 1),
            1.0,
            0.0,
        ).astype(F32)

    def chol_end(k):
        d = pl.ds(k * PB, PB)
        x = xblk[...]
        if k:
            left = pl.ds(0, k * PB)
            linv_ref[d, left] = -product(x, product(g_ref[d, left], linv_ref[left, left]))
        linv_ref[d, d] = x
        if k < PANELS - 1:
            rest = pl.ds((k + 1) * PB, (PANELS - 1 - k) * PB)
            below = tdot(g_ref[rest, d], x)
            g_ref[rest, d] = below
            g_ref[rest, rest] = g_ref[rest, rest] - tdot(below, below)

    pieces = []
    for k in range(PANELS):
        for q in range(PIECES):
            pieces.append((k, q))

    def piece(k, q):
        if q == 0:
            chol_begin(k)
        chol_steps(dblk, xblk, q * (PB // PIECES), (q + 1) * (PB // PIECES))
        if q == PIECES - 1:
            chol_end(k)

    summed = []
    emits = []

    def emit(c):
        slot = len(emits) % 2
        if len(emits) > 1:
            emits[-2].wait()
        cols = pl.ds(*chunks[c])
        top = pl.ds(0, HALF)
        low = pl.ds(HALF, HALF)
        fh, fl = split(f_ref[:, cols])
        u_ref[slot, top] = dot3(lh[top, top], ll[top, top], fh[:HALF], fl[:HALF])
        u_ref[slot, low] = dot3(lh[low, :], ll[low, :], fh, fl)
        out = pltpu.make_async_copy(
            u_ref.at[slot], f_out.at[:, pl.ds((c - 1) * CW, CW)], local_sem.at[2 + c]
        )
        out.start()
        emits.append(out)

    def ready_factor():
        hi, lo = split(linv_ref[...])
        lh[...] = hi
        ll[...] = lo

    steps = [(GRAM_TAU[p], 0, p) for p in range(7)]
    steps += [(2 * p + c, c, p) for c in range(1, n) for p in range(11)]
    before = None
    ready = False
    for tau, c, p in sorted(steps):
        if ready and tau != before and pieces:
            piece(*pieces.pop(0))
            if not pieces:
                ready_factor()
        elif ready and tau != before:
            for done in summed:
                emit(done)
            summed.clear()
        before = tau
        if c == 0:
            phase_gram(p)
        else:
            phase(c, p)
        ready = ready or (c, p) == (0, 6)
    for rest in pieces:
        piece(*rest)
    if pieces:
        ready_factor()
    for done in summed:
        emit(done)
    for out in emits[-2:]:
        out.wait()

    for copy in started.values():
        copy.wait_send()
    for band in range(len(bands)):
        over_peers(lambda k: mail(band, k).wait_send())
    for way in range(2):
        end = deep - 1 if way == 0 else 1

        @pl.when(z != end)
        def _():
            for q in range(na + nb):
                pass_on(way, q).wait_send()

    a1_save.wait()
    for save in saves:
        save.wait()


def all_reduced(front, child, owner, offset):
    rows, cols = front.shape
    kids = child.shape[0]
    count, deep = lax.axis_size("row"), lax.axis_size("col")
    wide = cols + WIDE
    n = 1 + cols // CW
    vm = pl.BlockSpec(memory_space=pltpu.VMEM)
    hbm = pl.BlockSpec(memory_space=pl.ANY)
    dma = pltpu.SemaphoreType.DMA
    box = TAG + cols // 2
    rings = rows // 2 // ZROWS + 4 * count // BROWS
    return pl.pallas_call(
        main_kernel,
        out_shape=(
            jax.ShapeDtypeStruct((rows, cols), F32),
            jax.ShapeDtypeStruct((WIDE, cols), F32),
            jax.ShapeDtypeStruct((rows, WIDE), F32),
            jax.ShapeDtypeStruct((WIDE, WIDE), F32),
        ),
        in_specs=[vm, vm, vm, vm, hbm],
        out_specs=(hbm, hbm, hbm, vm),
        scratch_shapes=[
            pltpu.VMEM((rows, cols), F32),
            pltpu.VMEM((WIDE, wide), F32),
            pltpu.VMEM((WIDE, wide), F32),
            pltpu.VMEM((rows, WIDE), F32),
            pltpu.VMEM((rows, WIDE), F32),
            pltpu.VMEM((WIDE, rows), BF16),
            pltpu.VMEM((WIDE, rows), BF16),
            pltpu.VMEM((HALF, wide), F32),
            pltpu.VMEM((6 * SHARD // 2, wide), F32),
            pltpu.VMEM((6 * SUB // 2, wide), F32),
            pltpu.VMEM((WIDE, WIDE), F32),
            pltpu.VMEM((PB, PB), F32),
            pltpu.VMEM((PB, PB), F32),
            pltpu.VMEM((8 * count, box), F32),
            pltpu.VMEM((8 * count, box), F32),
            pltpu.VMEM((8 * count, HC), F32),
            pltpu.VMEM((2, rows, 8 * count), BF16),
            pltpu.VMEM((WIDE, WIDE), BF16),
            pltpu.VMEM((WIDE, WIDE), BF16),
            pltpu.VMEM((2, WIDE, CW), F32),
            dma((n, COPIES)),
            dma((n, COPIES)),
            dma((3, count)),
            dma((3, count)),
            dma((2, rings)),
            dma((2, rings)),
            dma((2 + n,)),
        ],
        compiler_params=pltpu.CompilerParams(
            collective_id=0, has_side_effects=True, vmem_limit_bytes=63 * 1024 * 1024
        ),
        name="assemble_and_reduce",
    )(
        child,
        owner,
        owner.reshape(1, kids),
        offset.reshape(1, kids).astype(F32),
        front,
    )


def tail_kernel(scale, a1_ref, linv_ref, s_ref, w_ref, u_ref, o_ref, q_ref, qh, ql):
    @pl.when(pl.program_id(0) == 0)
    def _():
        basis = tdot(a1_ref[...], linv_ref[...])
        q_ref[...] = basis * scale
        hi, lo = split(basis)
        qh[...] = hi
        ql[...] = lo

    u = s_ref[...]
    u_ref[...] = u
    uh, ul = split(u)
    o_ref[...] = w_ref[...] - dot3(qh[...], ql[...], uh, ul)


def tail(a1, linv, upper, w, scale):
    rows, cols = w.shape
    tc = 512
    whole = lambda shape: pl.BlockSpec(shape, lambda i: (0, 0))
    tile = lambda size: pl.BlockSpec((size, tc), lambda i: (0, i))
    return pl.pallas_call(
        functools.partial(tail_kernel, scale),
        grid=(cols // tc,),
        out_shape=(
            jax.ShapeDtypeStruct((WIDE, cols), F32),
            jax.ShapeDtypeStruct((rows, cols), F32),
            jax.ShapeDtypeStruct((rows, WIDE), F32),
        ),
        in_specs=[whole((rows, WIDE)), whole((WIDE, WIDE)), tile(WIDE), tile(rows)],
        out_specs=(tile(WIDE), tile(rows), whole((rows, WIDE))),
        scratch_shapes=[pltpu.VMEM((rows, WIDE), BF16), pltpu.VMEM((rows, WIDE), BF16)],
        compiler_params=pltpu.CompilerParams(vmem_limit_bytes=62 * 1024 * 1024),
        name="project_out",
    )(a1, linv, upper, w)


def on_device(front_matrix, child_rows, child_owner, child_offset):
    total_rows = front_matrix.shape[0] * lax.axis_size("row")
    current, upper, panel, linv = all_reduced(front_matrix, child_rows, child_owner, child_offset)
    return tail(panel, linv, upper, current, math.sqrt(total_rows))


def solution(mesh):
    placed = (P("row", "col"), P("row", "col"), P("row", None), P("row", None))
    return jax.shard_map(
        on_device,
        mesh=mesh,
        in_specs=placed,
        out_specs=(P(None, "col"), P("row", "col"), P("row", None)),
        check_vma=False,
    )
```

```python
import functools
import math

import jax
import jax.numpy as jnp
from jax import lax
from jax.experimental import pallas as pl
from jax.experimental.pallas import tpu as pltpu
from jax.sharding import PartitionSpec as P

PB = 128
PANELS = 4
WIDE = PB * PANELS
MESH = pl.DeviceIdType.MESH
F32 = jnp.float32
BF16 = jnp.bfloat16
SIDE = 4
HALF = WIDE // 2
SHARD = HALF // SIDE
SUB = SHARD // SIDE
CW = 512
HC = 256
TAG = 128
GROUP = 4
PIECES = 4
GRAM_TAU = (-2, 0, 2, 4, 5.5, 7.5, 8.5)
COPIES = 22
ZROWS = 32
BROWS = 64


def product(left_op, right_op):
    return jnp.dot(
        left_op, right_op, precision=lax.Precision.HIGHEST, preferred_element_type=F32
    )


def split(value):
    high = value.astype(BF16)
    return high, (value - high.astype(F32)).astype(BF16)


def split3(value):
    high = value.astype(BF16)
    rest = value - high.astype(F32)
    mid = rest.astype(BF16)
    return high, mid, (rest - mid.astype(F32)).astype(BF16)


def place(onehot, value):
    high, mid, low = split3(value)

    def one(part):
        return jnp.dot(onehot, part, preferred_element_type=F32)

    return one(high) + (one(mid) + one(low))


def dot3(lh, ll, rh, rl):
    def one(a, b):
        return jnp.dot(a, b, preferred_element_type=F32)

    return one(lh, rh) + (one(lh, rl) + one(ll, rh))


def chol_steps(dblk, xblk, start, stop):
    live = pl.ds(start, PB - start)
    lane = lax.broadcasted_iota(jnp.int32, (PB - start, PB), 1)
    lane1 = lax.broadcasted_iota(jnp.int32, (1, PB), 1)
    sub = lax.broadcasted_iota(jnp.int32, (PB - start, PB), 0) + start

    def step(i, carry):
        j = i * GROUP
        a, x = dblk[live, :], xblk[live, :]
        span = range(GROUP)
        rows = [dblk[pl.ds(j + q, 1), :] for q in span]
        xrows = [xblk[pl.ds(j + q, 1), :] for q in span]
        cols = [
            jnp.sum(jnp.where(lane == j + q, a, 0.0), axis=1, keepdims=True) for q in span
        ]
        m = {
            (p, q): jnp.sum(jnp.where(lane1 == j + q, rows[p], 0.0), axis=1, keepdims=True)
            for p in span
            for q in range(p, GROUP)
        }
        invs = []
        for p in span:
            inv = lax.rsqrt(m[p, p])
            inv2 = inv * inv
            invs.append(inv)
            for q in range(p + 1, GROUP):
                f = m[p, q] * inv2
                rows[q] = rows[q] - f * rows[p]
                xrows[q] = xrows[q] - f * xrows[p]
                cols[q] = cols[q] - f * cols[p]
                for r in range(q, GROUP):
                    m[q, r] = m[q, r] - f * m[p, r]
            cols[p] = cols[p] * inv2
        below = sub > j + GROUP - 1
        na, nx = a, x
        for p in span:
            na = na - cols[p] * rows[p]
            nx = nx - cols[p] * xrows[p]
        nx = jnp.where(below, nx, x)
        for p in span:
            nx = jnp.where(sub == j + p, xrows[p] * invs[p], nx)
        dblk[live, :] = jnp.where(below, na, a)
        xblk[live, :] = nx
        return carry

    lax.fori_loop(start // GROUP, stop // GROUP, step, 0)


def tdot(a, b):
    return lax.dot_general(
        a, b, (((1,), (1,)), ((), ())), precision=lax.Precision.HIGHEST, preferred_element_type=F32
    )


def main_kernel(
    child_ref, ocol_ref, orow_ref, off_ref, front_ref,
    w_out, f_out, q_ref, linv_ref,
    w_ref, f_ref, p_ref, a1_ref, a1_full, ah, al, r0, r1, r2, g_ref, dblk, xblk,
    outbox, inbox, zbox, onehot,
    send_sem, recv_sem, box_send, box_recv, z_send, z_recv, local_sem,
):
    count = lax.axis_size("row")
    deep = lax.axis_size("col")
    r = lax.axis_index("row")
    z = lax.axis_index("col")
    core = lax.rem(r, 2)
    yy = lax.rem(r // 2, SIDE)
    xx = r // (2 * SIDE)
    other = 1 - core
    a = other * xx + core * yy
    b = core * xx + other * yy
    rows, total_cols = w_ref.shape
    kids = child_ref.shape[0]

    def mult8(v, m=8):
        return pl.multiple_of(v, m)

    def at(first, second):
        px = other * first + core * second
        py = core * first + other * second
        return (px * SIDE + py) * 2 + core

    first = pltpu.make_async_copy(front_ref.at[:, pl.ds(0, WIDE)], a1_ref, local_sem.at[1])

    @pl.when(z == 0)
    def _():
        first.start()

    load = pltpu.make_async_copy(front_ref, w_ref, local_sem.at[0])
    load.start()

    barrier = pltpu.get_barrier_semaphore()

    def greet(d, carry):
        pl.semaphore_signal(
            barrier, inc=1, device_id={"row": lax.rem(r + d, count)}, device_id_type=MESH
        )
        return carry

    lax.fori_loop(1, count, greet, 0)
    z_up, z_dn = lax.rem(z + 1, deep), lax.rem(z + deep - 1, deep)
    for peer in (z_up, z_dn):
        pl.semaphore_signal(barrier, inc=1, device_id={"col": peer}, device_id_type=MESH)

    orow = orow_ref[...]
    earlier = lax.broadcasted_iota(jnp.int32, (kids, kids), 0) < lax.broadcasted_iota(
        jnp.int32, (kids, kids), 1
    )
    same = jnp.logical_and(ocol_ref[...] == orow, earlier)
    rank = jnp.sum(jnp.where(same, 1.0, 0.0), axis=0, keepdims=True).astype(jnp.int32)
    slot = orow * 8 + rank * 2
    boxes = 8 * count
    box_id = lax.broadcasted_iota(jnp.int32, (boxes, kids), 0)
    even = jnp.where(box_id == slot, 1.0, 0.0)
    odd = jnp.where(box_id == slot + 1, 1.0, 0.0)
    filled = even + odd
    offset = jnp.sum(filled * off_ref[...], axis=1, keepdims=True)
    offset = offset + jnp.sum(filled, axis=1, keepdims=True) - 1.0
    outbox[:, pl.ds(0, TAG)] = jnp.broadcast_to(offset, (boxes, TAG))
    choose = jnp.concatenate([even, odd], axis=1).astype(BF16)

    def pack(m):
        lo = pl.multiple_of(m * 2 * HC, HC)
        both = jnp.concatenate(
            [child_ref[:, pl.ds(lo, HC)], child_ref[:, pl.ds(pl.multiple_of(lo + HC, HC), HC)]],
            axis=0,
        )
        outbox[:, pl.ds(pl.multiple_of(TAG + m * HC, TAG), HC)] = place(choose, both)

    nblk = total_cols // (2 * HC)
    bands = [
        (0, TAG + HC),
        (TAG + HC, 3 * HC),
        (TAG + 4 * HC, (nblk - 4) * HC),
    ]

    peers = [
        (dx, dy, dc)
        for dc in (1, 0)
        for dy in range(SIDE)
        for dx in (1, 3, 2, 0)
        if (dx, dy, dc) != (0, 0, 0)
    ]
    turn = 1 - 2 * core

    def mail(band, k):
        dx, dy, dc = peers[k]
        px = lax.rem(xx + turn * dx + SIDE, SIDE)
        py = lax.rem(yy + turn * dy + SIDE, SIDE)
        peer = (px * SIDE + py) * 2 + lax.rem(core + dc, 2)
        cols = pl.ds(*bands[band])
        return pltpu.make_async_remote_copy(
            src_ref=outbox.at[pl.ds(mult8(8 * peer), 8), cols],
            dst_ref=inbox.at[pl.ds(mult8(8 * r), 8), cols],
            send_sem=box_send.at[band, k],
            recv_sem=box_recv.at[band, k],
            device_id={"row": peer},
            device_id_type=MESH,
        )

    def over_peers(action):
        for k in range(len(peers)):
            action(k)

    def post(band):
        over_peers(lambda k: mail(band, k).start())
        mine = pl.ds(mult8(8 * r), 8)
        cols = pl.ds(*bands[band])
        inbox[mine, cols] = outbox[mine, cols]

    def collect(band):
        over_peers(lambda k: mail(band, k).wait_recv())

    na, nb = rows // 2 // ZROWS, boxes // 2 // BROWS

    def pass_on(way, q):
        if q < na:
            piece = a1_ref.at[pl.ds((way * na + q) * ZROWS, ZROWS), :]
        else:
            piece = zbox.at[pl.ds((way * nb + q - na) * BROWS, BROWS), :]
        return pltpu.make_async_remote_copy(
            src_ref=piece,
            dst_ref=piece,
            send_sem=z_send.at[way, q],
            recv_sem=z_recv.at[way, q],
            device_id={"col": z_up if way == 0 else z_dn},
            device_id_type=MESH,
        )

    def source(span):
        @pl.when(z == 0)
        def _():
            for q in span:
                for way in range(2):
                    pass_on(way, q).start()

    def near(span):
        for way in range(2):
            @pl.when(z == (1 if way == 0 else deep - 1))
            def _():
                for q in span:
                    pass_on(way, q).wait_recv()
                    pass_on(way, q).start()

        @pl.when(z == 2)
        def _():
            for q in span:
                for way in range(2):
                    pass_on(way, q).wait_recv()
                    pass_on(way, q).start()

    def far(span):
        for way in range(2):
            @pl.when(z == (1 if way == 1 else deep - 1))
            def _():
                for q in span:
                    pass_on(way, q).wait_recv()

    pack(0)

    @pl.when(z == 0)
    def _():
        first.wait()

    pl.semaphore_wait(barrier, count - 1 + 2)
    post(0)
    source(range(na))
    for m in range(1, 4):
        pack(m)
    post(1)
    for m in range(4, nblk):
        pack(m)
    post(2)
    near(range(na))

    collect(0)

    @pl.when(z == 0)
    def _():
        zbox[...] = inbox[:, pl.ds(TAG, HC)]

    source(range(na, na + nb))
    place_at = jnp.transpose(inbox[:, pl.ds(0, TAG)])[0:1, :]
    row_id = lax.broadcasted_iota(jnp.int32, (rows, boxes), 0).astype(F32)
    parity = lax.rem(lax.broadcasted_iota(jnp.int32, (rows, boxes), 1), 2)
    hit = row_id == place_at
    for h in range(2):
        onehot[h] = jnp.where(jnp.logical_and(hit, parity == h), 1.0, 0.0).astype(BF16)

    def assemble(m):
        value = inbox[:, pl.ds(pl.multiple_of(TAG + m * HC, TAG), HC)]
        high, mid, low = split3(value)
        for h in range(2):
            hot = onehot[h]
            cols = pl.ds(pl.multiple_of((2 * m + h) * HC, HC), HC)
            added = jnp.dot(hot, high, preferred_element_type=F32) + (
                jnp.dot(hot, mid, preferred_element_type=F32)
                + jnp.dot(hot, low, preferred_element_type=F32)
            )
            w_ref[:, cols] = w_ref[:, cols] + added

    near(range(na, na + nb))
    load.wait()
    assemble(0)
    far(range(na + nb))
    value = zbox[...]
    for h in range(2):
        cols = pl.ds(h * HC, HC)
        a1_full[:, cols] = a1_ref[:, cols] + place(onehot[h], value)

    a1t = jnp.transpose(a1_full[...])
    hi, lo = split(a1t)
    ah[...] = hi
    al[...] = lo
    p_ref[:, pl.ds(0, WIDE)] = product(a1t, a1_full[...])

    a_up, a_dn, a_op = lax.rem(a + 1, SIDE), lax.rem(a + 3, SIDE), lax.rem(a + 2, SIDE)
    b_up, b_dn, b_op = lax.rem(b + 1, SIDE), lax.rem(b + 3, SIDE), lax.rem(b + 2, SIDE)
    dev = {
        "p": r + 1 - 2 * core,
        "a+": at(a_up, b),
        "a-": at(a_dn, b),
        "ao": at(a_op, b),
        "b+": at(a, b_up),
        "b-": at(a, b_dn),
        "bo": at(a, b_op),
    }
    chunks = [(0, WIDE)] + [(WIDE + i * CW, CW) for i in range(total_cols // CW)]
    n = len(chunks)
    started = {}
    saves = []

    def send(c, slot, src, dst, where):
        copy = pltpu.make_async_remote_copy(
            src_ref=src,
            dst_ref=dst,
            send_sem=send_sem.at[c, slot],
            recv_sem=recv_sem.at[c, slot],
            device_id={"row": dev[where]},
            device_id_type=MESH,
        )
        copy.start()
        started[(c, slot)] = copy

    def got(c, *slots):
        for slot in slots:
            started[(c, slot)].wait_recv()

    own = HALF * core

    def shard(i, half=0):
        return mult8(own + SHARD * i + half * (SHARD // 2))

    def sub(i, half=0):
        return mult8(own + SHARD * a + SUB * i + half * (SUB // 2))

    s32, s8 = SHARD // 2, SUB // 2

    def fill(c):
        if c == 2:
            collect(1)
        if c == 5:
            collect(2)
        if c > 1:
            assemble(c - 1)
        if c == n - 1:
            save = pltpu.make_async_copy(w_ref, w_out, local_sem.at[2])
            save.start()
            saves.append(save)
        for i in range(CW // 256):
            off = (c - 1) * CW + i * 256
            wh, wl = split(w_ref[:, pl.ds(off, 256)])
            p_ref[:, pl.ds(off + WIDE, 256)] = dot3(ah[...], al[...], wh, wl)

    def tools(c):
        cols = pl.ds(*chunks[c])

        def part(row, size):
            return p_ref.at[pl.ds(row, size), cols]

        def full(row, size):
            return f_ref.at[pl.ds(row, size), cols]

        def add(row, size, *sources, into=p_ref):
            span = pl.ds(row, size)
            value = p_ref[span, cols]
            for source in sources:
                value = value + source[...]
            into[span, cols] = value

        def one(i, size=s32):
            return r1.at[pl.ds(i * size, size), cols]

        def two(i, size=s8):
            return r2.at[pl.ds(i * size, size), cols]

        return cols, part, full, add, one, two

    def phase_gram(p):
        c = 0
        cols, part, full, add, one, two = tools(c)
        if p == 0:
            send(c, 0, part(mult8(HALF * other), HALF), r0.at[:, cols], "p")
        elif p == 1:
            got(c, 0)
            add(mult8(own), HALF, r0.at[:, cols])
            send(c, 1, part(shard(a_op), SHARD), one(0, SHARD), "ao")
            send(c, 2, part(shard(a_up), SHARD), one(1, SHARD), "a+")
            send(c, 3, part(shard(a_dn), SHARD), one(2, SHARD), "a-")
        elif p == 2:
            got(c, 2, 3, 1)
            add(shard(a), SHARD, one(0, SHARD), one(1, SHARD), one(2, SHARD))
            send(c, 4, part(sub(b_op), SUB), two(0, SUB), "bo")
            send(c, 5, part(sub(b_up), SUB), two(1, SUB), "b+")
            send(c, 6, part(sub(b_dn), SUB), two(2, SUB), "b-")
        elif p == 3:
            got(c, 5, 6, 4)
            add(sub(b), SUB, two(0, SUB), two(1, SUB), two(2, SUB), into=f_ref)
            for slot, where in ((7, "bo"), (8, "b+"), (9, "b-")):
                send(c, slot, full(sub(b), SUB), full(sub(b), SUB), where)
        elif p == 4:
            got(c, 8, 9, 7)
            for slot, where in ((10, "ao"), (11, "a+"), (12, "a-")):
                send(c, slot, full(shard(a), SHARD), full(shard(a), SHARD), where)
        elif p == 5:
            got(c, 11, 12, 10)
            send(c, 13, full(mult8(own), HALF), full(mult8(own), HALF), "p")
        elif p == 6:
            got(c, 13)

    def phase(c, p):
        cols, part, full, add, one, two = tools(c)
        if p == 0:
            fill(c)
            send(c, 0, part(mult8(HALF * other), HALF), r0.at[:, cols], "p")
        elif p == 1:
            got(c, 0)
            add(mult8(own), HALF, r0.at[:, cols])
            send(c, 1, part(shard(a_op, 0), s32), one(0), "a+")
            send(c, 2, part(shard(a_op, 1), s32), one(1), "a-")
            send(c, 3, part(shard(a_up, 1), s32), one(2), "a+")
            send(c, 4, part(shard(a_dn, 0), s32), one(3), "a-")
        elif p == 2:
            got(c, 1)
            add(shard(a_up, 0), s32, one(0))
            send(c, 5, part(shard(a_up, 0), s32), one(4), "a+")
            got(c, 2)
            add(shard(a_dn, 1), s32, one(1))
            send(c, 6, part(shard(a_dn, 1), s32), one(5), "a-")
        elif p == 3:
            got(c, 3, 4, 5, 6)
            add(shard(a, 0), s32, one(3), one(4))
            add(shard(a, 1), s32, one(2), one(5))
            send(c, 7, part(sub(b_op), SUB), two(0, SUB), "bo")
            send(c, 8, part(sub(b_up), SUB), two(1, SUB), "b+")
            send(c, 9, part(sub(b_dn), SUB), two(2, SUB), "b-")
        elif p == 5:
            got(c, 8, 9, 7)
            add(sub(b), SUB, two(0, SUB), two(1, SUB), two(2, SUB), into=f_ref)
            for slot, where in ((13, "bo"), (14, "b+"), (15, "b-")):
                send(c, slot, full(sub(b), SUB), full(sub(b), SUB), where)
        elif p == 7:
            got(c, 14, 15, 13)
            send(c, 17, full(shard(a), SHARD), full(shard(a), SHARD), "a+")
            send(c, 18, full(shard(a), SHARD), full(shard(a), SHARD), "a-")
        elif p == 8:
            got(c, 17)
            send(c, 19, full(shard(a_dn, 0), s32), full(shard(a_dn, 0), s32), "a+")
            got(c, 18)
            send(c, 20, full(shard(a_up, 1), s32), full(shard(a_up, 1), s32), "a-")
        elif p == 9:
            got(c, 19, 20)
            send(c, 21, full(mult8(own), HALF), full(mult8(own), HALF), "p")
        elif p == 10:
            got(c, 21)
            save = pltpu.make_async_copy(
                f_ref.at[:, cols], f_out.at[:, pl.ds((c - 1) * CW, CW)], local_sem.at[2 + c]
            )
            save.start()
            saves.append(save)

    def chol_begin(k):
        if k == 0:
            g_ref[...] = f_ref[:, pl.ds(0, WIDE)]
            linv_ref[...] = jnp.zeros_like(linv_ref)
        d = pl.ds(k * PB, PB)
        dblk[...] = g_ref[d, d]
        xblk[...] = jnp.where(
            lax.broadcasted_iota(jnp.int32, (PB, PB), 0)
            == lax.broadcasted_iota(jnp.int32, (PB, PB), 1),
            1.0,
            0.0,
        ).astype(F32)

    def chol_end(k):
        d = pl.ds(k * PB, PB)
        x = xblk[...]
        if k:
            left = pl.ds(0, k * PB)
            linv_ref[d, left] = -product(x, product(g_ref[d, left], linv_ref[left, left]))
        linv_ref[d, d] = x
        if k < PANELS - 1:
            rest = pl.ds((k + 1) * PB, (PANELS - 1 - k) * PB)
            below = tdot(g_ref[rest, d], x)
            g_ref[rest, d] = below
            g_ref[rest, rest] = g_ref[rest, rest] - tdot(below, below)

    pieces = []
    for k in range(PANELS):
        for q in range(PIECES):
            pieces.append((k, q))

    def piece(k, q):
        if q == 0:
            chol_begin(k)
        chol_steps(dblk, xblk, q * (PB // PIECES), (q + 1) * (PB // PIECES))
        if q == PIECES - 1:
            chol_end(k)

    def ready_factor():
        q_ref[...] = tdot(a1_full[...], linv_ref[...])

    steps = [(GRAM_TAU[p], 0, p) for p in range(7)]
    steps += [(2 * p + c - 1, c, p) for c in range(1, n) for p in (0, 1, 2, 3, 5, 7, 8, 9, 10)]
    before = None
    ready = False
    for tau, c, p in sorted(steps):
        if ready and tau != before and pieces:
            piece(*pieces.pop(0))
            if not pieces:
                ready_factor()
        before = tau
        if c == 0:
            phase_gram(p)
        else:
            phase(c, p)
        ready = ready or (c, p) == (0, 6)
    for rest in pieces:
        piece(*rest)
    if pieces:
        ready_factor()

    for copy in started.values():
        copy.wait_send()
    for band in range(len(bands)):
        over_peers(lambda k: mail(band, k).wait_send())
    for way in range(2):
        end = deep - 1 if way == 0 else 1

        @pl.when(z != end)
        def _():
            for q in range(na + nb):
                pass_on(way, q).wait_send()

    for save in saves:
        save.wait()


def all_reduced(front, child, owner, offset):
    rows, cols = front.shape
    kids = child.shape[0]
    count, deep = lax.axis_size("row"), lax.axis_size("col")
    wide = cols + WIDE
    n = 1 + cols // CW
    vm = pl.BlockSpec(memory_space=pltpu.VMEM)
    hbm = pl.BlockSpec(memory_space=pl.ANY)
    dma = pltpu.SemaphoreType.DMA
    box = TAG + cols // 2
    rings = rows // 2 // ZROWS + 4 * count // BROWS
    return pl.pallas_call(
        main_kernel,
        out_shape=(
            jax.ShapeDtypeStruct((rows, cols), F32),
            jax.ShapeDtypeStruct((WIDE, cols), F32),
            jax.ShapeDtypeStruct((rows, WIDE), F32),
            jax.ShapeDtypeStruct((WIDE, WIDE), F32),
        ),
        in_specs=[vm, vm, vm, vm, hbm],
        out_specs=(hbm, hbm, vm, vm),
        scratch_shapes=[
            pltpu.VMEM((rows, cols), F32),
            pltpu.VMEM((WIDE, wide), F32),
            pltpu.VMEM((WIDE, wide), F32),
            pltpu.VMEM((rows, WIDE), F32),
            pltpu.VMEM((rows, WIDE), F32),
            pltpu.VMEM((WIDE, rows), BF16),
            pltpu.VMEM((WIDE, rows), BF16),
            pltpu.VMEM((HALF, wide), F32),
            pltpu.VMEM((6 * SHARD // 2, wide), F32),
            pltpu.VMEM((6 * SUB // 2, wide), F32),
            pltpu.VMEM((WIDE, WIDE), F32),
            pltpu.VMEM((PB, PB), F32),
            pltpu.VMEM((PB, PB), F32),
            pltpu.VMEM((8 * count, box), F32),
            pltpu.VMEM((8 * count, box), F32),
            pltpu.VMEM((8 * count, HC), F32),
            pltpu.VMEM((2, rows, 8 * count), BF16),
            dma((n, COPIES)),
            dma((n, COPIES)),
            dma((3, count)),
            dma((3, count)),
            dma((2, rings)),
            dma((2, rings)),
            dma((2 + n,)),
        ],
        compiler_params=pltpu.CompilerParams(
            collective_id=0, has_side_effects=True, vmem_limit_bytes=63 * 1024 * 1024
        ),
        name="assemble_and_reduce",
    )(
        child,
        owner,
        owner.reshape(1, kids),
        offset.reshape(1, kids).astype(F32),
        front,
    )


def tail_kernel(scale, basis_ref, linv_ref, s_ref, w_ref, u_ref, o_ref, q_ref, qh, ql, lh, ll):
    @pl.when(pl.program_id(0) == 0)
    def _():
        basis = basis_ref[...]
        q_ref[...] = basis * scale
        qh[...], ql[...] = split(basis)
        lh[...], ll[...] = split(linv_ref[...])

    fh, fl = split(s_ref[...])
    top, low = pl.ds(0, HALF), pl.ds(HALF, HALF)
    u_ref[top, :] = dot3(lh[top, top], ll[top, top], fh[:HALF], fl[:HALF])
    u_ref[low, :] = dot3(lh[low, :], ll[low, :], fh, fl)
    uh, ul = split(u_ref[...])
    o_ref[...] = w_ref[...] - dot3(qh[...], ql[...], uh, ul)


def tail(basis, linv, sums, w, scale):
    rows, cols = w.shape
    tc = 512
    whole = lambda size: pl.BlockSpec((size, WIDE), lambda i: (0, 0))
    tile = lambda size: pl.BlockSpec((size, tc), lambda i: (0, i))
    return pl.pallas_call(
        functools.partial(tail_kernel, scale),
        grid=(cols // tc,),
        out_shape=(
            jax.ShapeDtypeStruct((WIDE, cols), F32),
            jax.ShapeDtypeStruct((rows, cols), F32),
            jax.ShapeDtypeStruct((rows, WIDE), F32),
        ),
        in_specs=[whole(rows), whole(WIDE), tile(WIDE), tile(rows)],
        out_specs=(tile(WIDE), tile(rows), whole(rows)),
        scratch_shapes=[
            pltpu.VMEM((rows, WIDE), BF16),
            pltpu.VMEM((rows, WIDE), BF16),
            pltpu.VMEM((WIDE, WIDE), BF16),
            pltpu.VMEM((WIDE, WIDE), BF16),
        ],
        compiler_params=pltpu.CompilerParams(vmem_limit_bytes=62 * 1024 * 1024),
        name="project_out",
    )(basis, linv, sums, w)


def on_device(front_matrix, child_rows, child_owner, child_offset):
    total_rows = front_matrix.shape[0] * lax.axis_size("row")
    current, sums, basis, linv = all_reduced(front_matrix, child_rows, child_owner, child_offset)
    return tail(basis, linv, sums, current, math.sqrt(total_rows))


def solution(mesh):
    placed = (P("row", "col"), P("row", "col"), P("row", None), P("row", None))
    return jax.shard_map(
        on_device,
        mesh=mesh,
        in_specs=placed,
        out_specs=(P(None, "col"), P("row", "col"), P("row", None)),
        check_vma=False,
    )
```

```python
import functools
import math

import jax
import jax.numpy as jnp
from jax import lax
from jax.experimental import pallas as pl
from jax.experimental.pallas import tpu as pltpu
from jax.sharding import PartitionSpec as P

PB = 128
PANELS = 4
WIDE = PB * PANELS
MESH = pl.DeviceIdType.MESH
F32 = jnp.float32
BF16 = jnp.bfloat16
SIDE = 4
HALF = WIDE // 2
SHARD = HALF // SIDE
SUB = SHARD // SIDE
CW = 512
HC = 256
TAG = 128
GROUP = 4
PIECES = 4
GRAM_TAU = (-2, 0, 2, 4, 5.5, 7.5, 8.5)
COPIES = 22
ZROWS = 32
BROWS = 64


def product(left_op, right_op):
    return jnp.dot(
        left_op, right_op, precision=lax.Precision.HIGHEST, preferred_element_type=F32
    )


def split(value):
    high = value.astype(BF16)
    return high, (value - high.astype(F32)).astype(BF16)


def split3(value):
    high = value.astype(BF16)
    rest = value - high.astype(F32)
    mid = rest.astype(BF16)
    return high, mid, (rest - mid.astype(F32)).astype(BF16)


def place(onehot, value):
    high, mid, low = split3(value)

    def one(part):
        return jnp.dot(onehot, part, preferred_element_type=F32)

    return one(high) + (one(mid) + one(low))


def dot3(lh, ll, rh, rl):
    def one(a, b):
        return jnp.dot(a, b, preferred_element_type=F32)

    return one(lh, rh) + (one(lh, rl) + one(ll, rh))


def chol_steps(dblk, xblk, start, stop):
    live = pl.ds(start, PB - start)
    lane = lax.broadcasted_iota(jnp.int32, (PB - start, PB), 1)
    lane1 = lax.broadcasted_iota(jnp.int32, (1, PB), 1)
    sub = lax.broadcasted_iota(jnp.int32, (PB - start, PB), 0) + start

    def step(i, carry):
        j = i * GROUP
        a, x = dblk[live, :], xblk[live, :]
        span = range(GROUP)
        rows = [dblk[pl.ds(j + q, 1), :] for q in span]
        xrows = [xblk[pl.ds(j + q, 1), :] for q in span]
        cols = [
            jnp.sum(jnp.where(lane == j + q, a, 0.0), axis=1, keepdims=True) for q in span
        ]
        m = {
            (p, q): jnp.sum(jnp.where(lane1 == j + q, rows[p], 0.0), axis=1, keepdims=True)
            for p in span
            for q in range(p, GROUP)
        }
        invs = []
        for p in span:
            inv = lax.rsqrt(m[p, p])
            inv2 = inv * inv
            invs.append(inv)
            for q in range(p + 1, GROUP):
                f = m[p, q] * inv2
                rows[q] = rows[q] - f * rows[p]
                xrows[q] = xrows[q] - f * xrows[p]
                cols[q] = cols[q] - f * cols[p]
                for r in range(q, GROUP):
                    m[q, r] = m[q, r] - f * m[p, r]
            cols[p] = cols[p] * inv2
        below = sub > j + GROUP - 1
        na, nx = a, x
        for p in span:
            na = na - cols[p] * rows[p]
            nx = nx - cols[p] * xrows[p]
        nx = jnp.where(below, nx, x)
        for p in span:
            nx = jnp.where(sub == j + p, xrows[p] * invs[p], nx)
        dblk[live, :] = jnp.where(below, na, a)
        xblk[live, :] = nx
        return carry

    lax.fori_loop(start // GROUP, stop // GROUP, step, 0)


def tdot(a, b):
    return lax.dot_general(
        a, b, (((1,), (1,)), ((), ())), precision=lax.Precision.HIGHEST, preferred_element_type=F32
    )


def main_kernel(
    child_ref, orow_ref, off_ref, front_ref,
    w_out, f_out, q_ref, linv_ref,
    w_ref, f_ref, p_ref, a1_ref, a1_full, ah, al, r0, r1, r2, g_ref, dblk, xblk,
    outbox, inbox, zbox, onehot,
    send_sem, recv_sem, box_send, box_recv, z_send, z_recv, local_sem,
):
    count = lax.axis_size("row")
    deep = lax.axis_size("col")
    r = lax.axis_index("row")
    z = lax.axis_index("col")
    core = lax.rem(r, 2)
    yy = lax.rem(r // 2, SIDE)
    xx = r // (2 * SIDE)
    other = 1 - core
    a = other * xx + core * yy
    b = core * xx + other * yy
    rows, total_cols = w_ref.shape
    kids = child_ref.shape[0]

    def mult8(v, m=8):
        return pl.multiple_of(v, m)

    def at(first, second):
        px = other * first + core * second
        py = core * first + other * second
        return (px * SIDE + py) * 2 + core

    first = pltpu.make_async_copy(front_ref.at[:, pl.ds(0, WIDE)], a1_ref, local_sem.at[1])

    @pl.when(z == 0)
    def _():
        first.start()

    load = pltpu.make_async_copy(front_ref, w_ref, local_sem.at[0])
    load.start()

    barrier = pltpu.get_barrier_semaphore()

    def greet(d, carry):
        pl.semaphore_signal(
            barrier, inc=1, device_id={"row": lax.rem(r + d, count)}, device_id_type=MESH
        )
        return carry

    lax.fori_loop(1, count, greet, 0)
    z_up, z_dn = lax.rem(z + 1, deep), lax.rem(z + deep - 1, deep)
    for peer in (z_up, z_dn):
        pl.semaphore_signal(barrier, inc=1, device_id={"col": peer}, device_id_type=MESH)

    orow = orow_ref[...]
    owner = orow.astype(F32)
    kid_down = lax.broadcasted_iota(jnp.int32, (kids, kids), 0)
    kid_over = lax.broadcasted_iota(jnp.int32, (kids, kids), 1)
    owner_down = jnp.sum(jnp.where(kid_down == kid_over, owner, 0.0), axis=1, keepdims=True)
    same = jnp.logical_and(owner_down == owner, kid_down < kid_over)
    rank = jnp.sum(jnp.where(same, 1.0, 0.0), axis=0, keepdims=True).astype(jnp.int32)
    slot = orow * 8 + rank * 2
    boxes = 8 * count
    box_id = lax.broadcasted_iota(jnp.int32, (boxes, kids), 0)
    even = jnp.where(box_id == slot, 1.0, 0.0)
    odd = jnp.where(box_id == slot + 1, 1.0, 0.0)
    filled = even + odd
    offset = jnp.sum(filled * off_ref[...].astype(F32), axis=1, keepdims=True)
    offset = offset + jnp.sum(filled, axis=1, keepdims=True) - 1.0
    outbox[:, pl.ds(0, TAG)] = jnp.broadcast_to(offset, (boxes, TAG))
    choose = jnp.concatenate([even, odd], axis=1).astype(BF16)

    def pack(m):
        lo = pl.multiple_of(m * 2 * HC, HC)
        both = jnp.concatenate(
            [child_ref[:, pl.ds(lo, HC)], child_ref[:, pl.ds(pl.multiple_of(lo + HC, HC), HC)]],
            axis=0,
        )
        outbox[:, pl.ds(pl.multiple_of(TAG + m * HC, TAG), HC)] = place(choose, both)

    nblk = total_cols // (2 * HC)
    bands = [
        (0, TAG + HC),
        (TAG + HC, 3 * HC),
        (TAG + 4 * HC, (nblk - 4) * HC),
    ]

    peers = [
        (dx, dy, dc)
        for dc in (1, 0)
        for dy in range(SIDE)
        for dx in (1, 3, 2, 0)
        if (dx, dy, dc) != (0, 0, 0)
    ]
    turn = 1 - 2 * core

    def mail(band, k):
        dx, dy, dc = peers[k]
        px = lax.rem(xx + turn * dx + SIDE, SIDE)
        py = lax.rem(yy + turn * dy + SIDE, SIDE)
        peer = (px * SIDE + py) * 2 + lax.rem(core + dc, 2)
        cols = pl.ds(*bands[band])
        return pltpu.make_async_remote_copy(
            src_ref=outbox.at[pl.ds(mult8(8 * peer), 8), cols],
            dst_ref=inbox.at[pl.ds(mult8(8 * r), 8), cols],
            send_sem=box_send.at[band, k],
            recv_sem=box_recv.at[band, k],
            device_id={"row": peer},
            device_id_type=MESH,
        )

    def over_peers(action):
        for k in range(len(peers)):
            action(k)

    def post(band):
        over_peers(lambda k: mail(band, k).start())
        mine = pl.ds(mult8(8 * r), 8)
        cols = pl.ds(*bands[band])
        inbox[mine, cols] = outbox[mine, cols]

    def collect(band):
        over_peers(lambda k: mail(band, k).wait_recv())

    na, nb = rows // 2 // ZROWS, boxes // 2 // BROWS

    def pass_on(way, q):
        if q < na:
            piece = a1_ref.at[pl.ds((way * na + q) * ZROWS, ZROWS), :]
        else:
            piece = zbox.at[pl.ds((way * nb + q - na) * BROWS, BROWS), :]
        return pltpu.make_async_remote_copy(
            src_ref=piece,
            dst_ref=piece,
            send_sem=z_send.at[way, q],
            recv_sem=z_recv.at[way, q],
            device_id={"col": z_up if way == 0 else z_dn},
            device_id_type=MESH,
        )

    def source(span):
        @pl.when(z == 0)
        def _():
            for q in span:
                for way in range(2):
                    pass_on(way, q).start()

    def near(span):
        for way in range(2):
            @pl.when(z == (1 if way == 0 else deep - 1))
            def _():
                for q in span:
                    pass_on(way, q).wait_recv()
                    pass_on(way, q).start()

        @pl.when(z == 2)
        def _():
            for q in span:
                for way in range(2):
                    pass_on(way, q).wait_recv()
                    pass_on(way, q).start()

    def far(span):
        for way in range(2):
            @pl.when(z == (1 if way == 1 else deep - 1))
            def _():
                for q in span:
                    pass_on(way, q).wait_recv()

    pack(0)

    @pl.when(z == 0)
    def _():
        first.wait()

    pl.semaphore_wait(barrier, count - 1 + 2)
    post(0)
    source(range(na))
    for m in range(1, 4):
        pack(m)
    post(1)
    for m in range(4, nblk):
        pack(m)
    post(2)
    near(range(na))

    collect(0)

    @pl.when(z == 0)
    def _():
        zbox[...] = inbox[:, pl.ds(TAG, HC)]

    source(range(na, na + nb))
    place_at = jnp.transpose(inbox[:, pl.ds(0, TAG)])[0:1, :]
    row_id = lax.broadcasted_iota(jnp.int32, (rows, boxes), 0).astype(F32)
    parity = lax.rem(lax.broadcasted_iota(jnp.int32, (rows, boxes), 1), 2)
    hit = row_id == place_at
    for h in range(2):
        onehot[h] = jnp.where(jnp.logical_and(hit, parity == h), 1.0, 0.0).astype(BF16)

    def assemble(m):
        value = inbox[:, pl.ds(pl.multiple_of(TAG + m * HC, TAG), HC)]
        high, mid, low = split3(value)
        for h in range(2):
            hot = onehot[h]
            cols = pl.ds(pl.multiple_of((2 * m + h) * HC, HC), HC)
            added = jnp.dot(hot, high, preferred_element_type=F32) + (
                jnp.dot(hot, mid, preferred_element_type=F32)
                + jnp.dot(hot, low, preferred_element_type=F32)
            )
            w_ref[:, cols] = w_ref[:, cols] + added

    near(range(na, na + nb))
    load.wait()
    assemble(0)
    far(range(na + nb))
    value = zbox[...]
    for h in range(2):
        cols = pl.ds(h * HC, HC)
        a1_full[:, cols] = a1_ref[:, cols] + place(onehot[h], value)

    a1t = jnp.transpose(a1_full[...])
    hi, lo = split(a1t)
    ah[...] = hi
    al[...] = lo
    p_ref[:, pl.ds(0, WIDE)] = product(a1t, a1_full[...])

    a_up, a_dn, a_op = lax.rem(a + 1, SIDE), lax.rem(a + 3, SIDE), lax.rem(a + 2, SIDE)
    b_up, b_dn, b_op = lax.rem(b + 1, SIDE), lax.rem(b + 3, SIDE), lax.rem(b + 2, SIDE)
    dev = {
        "p": r + 1 - 2 * core,
        "a+": at(a_up, b),
        "a-": at(a_dn, b),
        "ao": at(a_op, b),
        "b+": at(a, b_up),
        "b-": at(a, b_dn),
        "bo": at(a, b_op),
    }
    chunks = [(0, WIDE)] + [(WIDE + i * CW, CW) for i in range(total_cols // CW)]
    n = len(chunks)
    started = {}
    saves = []

    def send(c, slot, src, dst, where):
        copy = pltpu.make_async_remote_copy(
            src_ref=src,
            dst_ref=dst,
            send_sem=send_sem.at[c, slot],
            recv_sem=recv_sem.at[c, slot],
            device_id={"row": dev[where]},
            device_id_type=MESH,
        )
        copy.start()
        started[(c, slot)] = copy

    def got(c, *slots):
        for slot in slots:
            started[(c, slot)].wait_recv()

    own = HALF * core

    def shard(i, half=0):
        return mult8(own + SHARD * i + half * (SHARD // 2))

    def sub(i, half=0):
        return mult8(own + SHARD * a + SUB * i + half * (SUB // 2))

    s32, s8 = SHARD // 2, SUB // 2

    def fill(c):
        if c == 2:
            collect(1)
        if c == 5:
            collect(2)
        if c > 1:
            assemble(c - 1)
        if c == n - 1:
            save = pltpu.make_async_copy(w_ref, w_out, local_sem.at[2])
            save.start()
            saves.append(save)
        for i in range(CW // 256):
            off = (c - 1) * CW + i * 256
            wh, wl = split(w_ref[:, pl.ds(off, 256)])
            p_ref[:, pl.ds(off + WIDE, 256)] = dot3(ah[...], al[...], wh, wl)

    def tools(c):
        cols = pl.ds(*chunks[c])

        def part(row, size):
            return p_ref.at[pl.ds(row, size), cols]

        def full(row, size):
            return f_ref.at[pl.ds(row, size), cols]

        def add(row, size, *sources, into=p_ref):
            span = pl.ds(row, size)
            value = p_ref[span, cols]
            for source in sources:
                value = value + source[...]
            into[span, cols] = value

        def one(i, size=s32):
            return r1.at[pl.ds(i * size, size), cols]

        def two(i, size=s8):
            return r2.at[pl.ds(i * size, size), cols]

        return cols, part, full, add, one, two

    def phase_gram(p):
        c = 0
        cols, part, full, add, one, two = tools(c)
        if p == 0:
            send(c, 0, part(mult8(HALF * other), HALF), r0.at[:, cols], "p")
        elif p == 1:
            got(c, 0)
            add(mult8(own), HALF, r0.at[:, cols])
            send(c, 1, part(shard(a_op), SHARD), one(0, SHARD), "ao")
            send(c, 2, part(shard(a_up), SHARD), one(1, SHARD), "a+")
            send(c, 3, part(shard(a_dn), SHARD), one(2, SHARD), "a-")
        elif p == 2:
            got(c, 2, 3, 1)
            add(shard(a), SHARD, one(0, SHARD), one(1, SHARD), one(2, SHARD))
            send(c, 4, part(sub(b_op), SUB), two(0, SUB), "bo")
            send(c, 5, part(sub(b_up), SUB), two(1, SUB), "b+")
            send(c, 6, part(sub(b_dn), SUB), two(2, SUB), "b-")
        elif p == 3:
            got(c, 5, 6, 4)
            add(sub(b), SUB, two(0, SUB), two(1, SUB), two(2, SUB), into=f_ref)
            for slot, where in ((7, "bo"), (8, "b+"), (9, "b-")):
                send(c, slot, full(sub(b), SUB), full(sub(b), SUB), where)
        elif p == 4:
            got(c, 8, 9, 7)
            for slot, where in ((10, "ao"), (11, "a+"), (12, "a-")):
                send(c, slot, full(shard(a), SHARD), full(shard(a), SHARD), where)
        elif p == 5:
            got(c, 11, 12, 10)
            send(c, 13, full(mult8(own), HALF), full(mult8(own), HALF), "p")
        elif p == 6:
            got(c, 13)

    def phase(c, p):
        cols, part, full, add, one, two = tools(c)
        if p == 0:
            fill(c)
            send(c, 0, part(mult8(HALF * other), HALF), r0.at[:, cols], "p")
        elif p == 1:
            got(c, 0)
            add(mult8(own), HALF, r0.at[:, cols])
            send(c, 1, part(shard(a_op, 0), s32), one(0), "a+")
            send(c, 2, part(shard(a_op, 1), s32), one(1), "a-")
            send(c, 3, part(shard(a_up, 1), s32), one(2), "a+")
            send(c, 4, part(shard(a_dn, 0), s32), one(3), "a-")
        elif p == 2:
            got(c, 1)
            add(shard(a_up, 0), s32, one(0))
            send(c, 5, part(shard(a_up, 0), s32), one(4), "a+")
            got(c, 2)
            add(shard(a_dn, 1), s32, one(1))
            send(c, 6, part(shard(a_dn, 1), s32), one(5), "a-")
        elif p == 3:
            got(c, 3, 4, 5, 6)
            add(shard(a, 0), s32, one(3), one(4))
            add(shard(a, 1), s32, one(2), one(5))
            send(c, 7, part(sub(b_op), SUB), two(0, SUB), "bo")
            send(c, 8, part(sub(b_up), SUB), two(1, SUB), "b+")
            send(c, 9, part(sub(b_dn), SUB), two(2, SUB), "b-")
        elif p == 5:
            got(c, 8, 9, 7)
            add(sub(b), SUB, two(0, SUB), two(1, SUB), two(2, SUB), into=f_ref)
            for slot, where in ((13, "bo"), (14, "b+"), (15, "b-")):
                send(c, slot, full(sub(b), SUB), full(sub(b), SUB), where)
        elif p == 7:
            got(c, 14, 15, 13)
            send(c, 17, full(shard(a), SHARD), full(shard(a), SHARD), "a+")
            send(c, 18, full(shard(a), SHARD), full(shard(a), SHARD), "a-")
        elif p == 8:
            got(c, 17)
            send(c, 19, full(shard(a_dn, 0), s32), full(shard(a_dn, 0), s32), "a+")
            got(c, 18)
            send(c, 20, full(shard(a_up, 1), s32), full(shard(a_up, 1), s32), "a-")
        elif p == 9:
            got(c, 19, 20)
            send(c, 21, full(mult8(own), HALF), full(mult8(own), HALF), "p")
        elif p == 10:
            got(c, 21)
            save = pltpu.make_async_copy(
                f_ref.at[:, cols], f_out.at[:, pl.ds((c - 1) * CW, CW)], local_sem.at[2 + c]
            )
            save.start()
            saves.append(save)

    def chol_begin(k):
        if k == 0:
            g_ref[...] = f_ref[:, pl.ds(0, WIDE)]
            linv_ref[...] = jnp.zeros_like(linv_ref)
        d = pl.ds(k * PB, PB)
        dblk[...] = g_ref[d, d]
        xblk[...] = jnp.where(
            lax.broadcasted_iota(jnp.int32, (PB, PB), 0)
            == lax.broadcasted_iota(jnp.int32, (PB, PB), 1),
            1.0,
            0.0,
        ).astype(F32)

    def chol_end(k):
        d = pl.ds(k * PB, PB)
        x = xblk[...]
        if k:
            left = pl.ds(0, k * PB)
            linv_ref[d, left] = -product(x, product(g_ref[d, left], linv_ref[left, left]))
        linv_ref[d, d] = x
        if k < PANELS - 1:
            rest = pl.ds((k + 1) * PB, (PANELS - 1 - k) * PB)
            below = tdot(g_ref[rest, d], x)
            g_ref[rest, d] = below
            g_ref[rest, rest] = g_ref[rest, rest] - tdot(below, below)

    pieces = []
    for k in range(PANELS):
        for q in range(PIECES):
            pieces.append((k, q))

    def piece(k, q):
        if q == 0:
            chol_begin(k)
        chol_steps(dblk, xblk, q * (PB // PIECES), (q + 1) * (PB // PIECES))
        if q == PIECES - 1:
            chol_end(k)

    def ready_factor():
        q_ref[...] = tdot(a1_full[...], linv_ref[...])

    steps = [(GRAM_TAU[p], 0, p) for p in range(7)]
    steps += [(1.5 * p + 0.75 * c - 1, c, p) for c in range(1, n) for p in (0, 1, 2, 3, 5, 7, 8, 9, 10)]
    before = None
    ready = False
    for tau, c, p in sorted(steps):
        if ready and tau != before and pieces:
            piece(*pieces.pop(0))
            if not pieces:
                ready_factor()
        before = tau
        if c == 0:
            phase_gram(p)
        else:
            phase(c, p)
        ready = ready or (c, p) == (0, 6)
    for rest in pieces:
        piece(*rest)
    if pieces:
        ready_factor()

    for copy in started.values():
        copy.wait_send()
    for band in range(len(bands)):
        over_peers(lambda k: mail(band, k).wait_send())
    for way in range(2):
        end = deep - 1 if way == 0 else 1

        @pl.when(z != end)
        def _():
            for q in range(na + nb):
                pass_on(way, q).wait_send()

    for save in saves:
        save.wait()


def all_reduced(front, child, owner, offset):
    rows, cols = front.shape
    kids = child.shape[0]
    count, deep = lax.axis_size("row"), lax.axis_size("col")
    wide = cols + WIDE
    n = 1 + cols // CW
    vm = pl.BlockSpec(memory_space=pltpu.VMEM)
    hbm = pl.BlockSpec(memory_space=pl.ANY)
    dma = pltpu.SemaphoreType.DMA
    box = TAG + cols // 2
    rings = rows // 2 // ZROWS + 4 * count // BROWS
    return pl.pallas_call(
        main_kernel,
        out_shape=(
            jax.ShapeDtypeStruct((rows, cols), F32),
            jax.ShapeDtypeStruct((WIDE, cols), F32),
            jax.ShapeDtypeStruct((rows, WIDE), F32),
            jax.ShapeDtypeStruct((WIDE, WIDE), F32),
        ),
        in_specs=[vm, vm, vm, hbm],
        out_specs=(hbm, hbm, vm, vm),
        scratch_shapes=[
            pltpu.VMEM((rows, cols), F32),
            pltpu.VMEM((WIDE, wide), F32),
            pltpu.VMEM((WIDE, wide), F32),
            pltpu.VMEM((rows, WIDE), F32),
            pltpu.VMEM((rows, WIDE), F32),
            pltpu.VMEM((WIDE, rows), BF16),
            pltpu.VMEM((WIDE, rows), BF16),
            pltpu.VMEM((HALF, wide), F32),
            pltpu.VMEM((6 * SHARD // 2, wide), F32),
            pltpu.VMEM((6 * SUB // 2, wide), F32),
            pltpu.VMEM((WIDE, WIDE), F32),
            pltpu.VMEM((PB, PB), F32),
            pltpu.VMEM((PB, PB), F32),
            pltpu.VMEM((8 * count, box), F32),
            pltpu.VMEM((8 * count, box), F32),
            pltpu.VMEM((8 * count, HC), F32),
            pltpu.VMEM((2, rows, 8 * count), BF16),
            dma((n, COPIES)),
            dma((n, COPIES)),
            dma((3, count)),
            dma((3, count)),
            dma((2, rings)),
            dma((2, rings)),
            dma((2 + n,)),
        ],
        compiler_params=pltpu.CompilerParams(
            collective_id=0, has_side_effects=True, vmem_limit_bytes=63 * 1024 * 1024
        ),
        name="assemble_and_reduce",
    )(
        child,
        owner.reshape(1, kids),
        offset.reshape(1, kids),
        front,
    )


def tail_kernel(scale, basis_ref, linv_ref, s_ref, w_ref, u_ref, o_ref, q_ref, qh, ql, lh, ll):
    @pl.when(pl.program_id(0) == 0)
    def _():
        basis = basis_ref[...]
        q_ref[...] = basis * scale
        qh[...], ql[...] = split(basis)
        lh[...], ll[...] = split(linv_ref[...])

    fh, fl = split(s_ref[...])
    top, low = pl.ds(0, HALF), pl.ds(HALF, HALF)
    u_ref[top, :] = dot3(lh[top, top], ll[top, top], fh[:HALF], fl[:HALF])
    u_ref[low, :] = dot3(lh[low, :], ll[low, :], fh, fl)
    uh, ul = split(u_ref[...])
    o_ref[...] = w_ref[...] - dot3(qh[...], ql[...], uh, ul)


def tail(basis, linv, sums, w, scale):
    rows, cols = w.shape
    tc = 1024
    whole = lambda size: pl.BlockSpec((size, WIDE), lambda i: (0, 0))
    tile = lambda size: pl.BlockSpec((size, tc), lambda i: (0, i))
    return pl.pallas_call(
        functools.partial(tail_kernel, scale),
        grid=(cols // tc,),
        out_shape=(
            jax.ShapeDtypeStruct((WIDE, cols), F32),
            jax.ShapeDtypeStruct((rows, cols), F32),
            jax.ShapeDtypeStruct((rows, WIDE), F32),
        ),
        in_specs=[whole(rows), whole(WIDE), tile(WIDE), tile(rows)],
        out_specs=(tile(WIDE), tile(rows), whole(rows)),
        scratch_shapes=[
            pltpu.VMEM((rows, WIDE), BF16),
            pltpu.VMEM((rows, WIDE), BF16),
            pltpu.VMEM((WIDE, WIDE), BF16),
            pltpu.VMEM((WIDE, WIDE), BF16),
        ],
        compiler_params=pltpu.CompilerParams(vmem_limit_bytes=62 * 1024 * 1024),
        name="project_out",
    )(basis, linv, sums, w)


def on_device(front_matrix, child_rows, child_owner, child_offset):
    total_rows = front_matrix.shape[0] * lax.axis_size("row")
    current, sums, basis, linv = all_reduced(front_matrix, child_rows, child_owner, child_offset)
    return tail(basis, linv, sums, current, math.sqrt(total_rows))


def solution(mesh):
    placed = (P("row", "col"), P("row", "col"), P("row", None), P("row", None))
    return jax.shard_map(
        on_device,
        mesh=mesh,
        in_specs=placed,
        out_specs=(P(None, "col"), P("row", "col"), P("row", None)),
        check_vma=False,
    )
```
